512 devices in a mesh: dp: 32 (over z, y_lo), seq: 16 (over x, y_hi, core).
Axes of the slice: x: 4, y: 8 (y_hi: 2, y_lo: 4; y = y_hi * 4 + y_lo), z: 8, core: 2. Of those that a mesh axis runs over, the one named last changes fastest.
Arguments:
- bases: int32 [32, 24576], P('dp', 'seq'), may hold values from 0 to 3
- embed_weight: bfloat16 [15, 4, 768], P(None, None, 'dp'), may hold values from -1.5 to 1.5
- embed_bias: bfloat16 [768], P('dp'), may hold values from -3 to 3
- norm_gain: bfloat16 [768], P('dp'), may hold values from 0.5 to 1.5
- proj_weight: bfloat16 [768, 896], P('dp'), may hold values from -0.21875 to 0.21875
- proj_bias: bfloat16 [896], P('dp'), may hold values from -3 to 3
- cotangent: bfloat16 [32, 12288, 896], P('dp', 'seq'), may hold values from -6 to 6
Outputs:
- pooled: bfloat16 [32, 12288, 896], P('dp', 'seq')
- grad_embed_weight: float32 [15, 4, 768], P(None, None, 'dp')
- grad_embed_bias: float32 [768], P('dp')
- grad_norm_gain: float32 [768], P('dp')
- grad_proj_weight: float32 [768, 896], P('dp')
- grad_proj_bias: float32 [896], P('dp')
The draws below stay inside these ranges and needn't reach their ends.
All inputs are finite; a program needn't handle non-finite values.
Results may differ from the reference program's by a relative error of at most 0.0065.
Values may be sent and summed in bfloat16 or wider, within the bound.
No kernel may reach another device: no remote copies, remote signals or barrier semaphores. Data moves between devices by JAX's collectives and lax.ppermute only.
A program may use at most 64 MiB of HBM per device.

```python
import jax
import jax.numpy as jnp
from jax import lax

D0 = 768
D1 = 896
KW = 15
SEQ = 24576
BATCH = 32


def plant(result, own_key, smallest, largest):
    dims = result.shape
    place = [jax.random.randint(jax.random.fold_in(own_key, axis), (), 0, dims[axis]) for axis in range(len(dims))]
    result = result.at[tuple(place)].set(smallest)
    longest = dims.index(max(dims))
    place[longest] = (place[longest] + 1) % dims[longest]
    return result.at[tuple(place)].set(largest)


def raised(result, key, source, target, shards_of, factor):
    def block_of(position):
        return (jnp.arange(result.shape[position]) // (result.shape[position] // shards_of)).reshape((-1,) + (1,) * (result.ndim - 1 - position))

    one_side = jax.random.permutation(key, shards_of)[block_of(target)]
    second = (block_of(target) + shards_of // 2) % shards_of
    return jnp.where((block_of(source) == one_side) | (block_of(source) == second), factor * result, result)


def levels(own_key, shape, split, least, high):
    level, own = 1.0, jax.random.fold_in(own_key, 6)
    for axis_at, blocks in split:
        draws = jnp.exp(jax.random.uniform(jax.random.fold_in(own, axis_at), (blocks,), jnp.float32, least / len(split), high / len(split)))
        level = level * jnp.repeat(draws, shape[axis_at] // blocks).reshape([-1 if axis == axis_at else 1 for axis in range(len(shape))])
    return level


def scatter_about(stream_key, dims, spread, reach, pieces=(), kind=jnp.bfloat16):
    drawn = jax.random.normal(stream_key, dims, jnp.float32) * spread
    if len(pieces) > 0:
        drawn = levels(stream_key, dims, pieces, -0.22, 0.18) * drawn
    return jnp.clip(drawn, min=-reach, max=reach).astype(kind)


def heavy_noise(rng, shape, spread, most, cuts, heavy, held_as=jnp.bfloat16):
    drawn = spread * jax.random.normal(rng, shape, jnp.float32)
    if cuts:
        drawn = drawn * levels(rng, shape, cuts, -0.22, 0.18)
    return jnp.clip(raised(drawn, jax.random.fold_in(rng, 3), *heavy), -most, most).astype(held_as)


def setup_inputs(seed: int = 0) -> dict:
    arg_keys = jax.random.split(jax.random.key(seed), 8)
    return {
        "bases": plant(jax.random.randint(arg_keys[0], (BATCH, SEQ), 0, 4), jax.random.fold_in(arg_keys[0], 1), 0, 3).astype(jnp.int32),
        "embed_weight": scatter_about(arg_keys[1], (KW, 4, D0), KW ** -0.5, 1.5, ((2, 32),)),
        "embed_bias": scatter_about(arg_keys[2], (D0,), 0.5, 3.0, ((0, 32),)),
        "norm_gain": jnp.clip(1.0 + 0.1 * jax.random.normal(arg_keys[3], (D0,), jnp.float32), 0.5, 1.5).astype(jnp.bfloat16),
        "proj_weight": scatter_about(arg_keys[4], (D0, D1), D0 ** -0.5, 0.21875, ((0, 32),)),
        "proj_bias": scatter_about(arg_keys[5], (D1,), 0.5, 3.0, ((0, 32),)),
        "cotangent": heavy_noise(arg_keys[6], (BATCH, SEQ // 2, D1), 1.0, 6.0, ((0, 32), (1, 16)), (0, 2, 32, 2.75)),
    }


def sample_pass(codes, cotan, embed_weight, embed_bias, norm_gain, proj_weight, proj_bias, scale_factor):
    kernel_width = embed_weight.shape[0]
    row_count = cotan.shape[0] * 2
    letters = jnp.arange(1, 5, dtype=jnp.int32)
    features = jnp.concatenate([(codes[k:k + row_count, None] == letters).astype(jnp.bfloat16) for k in range(kernel_width)], axis=1)
    flat_weight = embed_weight.reshape(kernel_width * 4, -1)
    embedded = (jnp.dot(features, flat_weight, preferred_element_type=jnp.float32) + embed_bias.astype(jnp.float32)).astype(jnp.bfloat16)
    values = embedded.astype(jnp.float32)
    inverse = lax.rsqrt(lax.optimization_barrier(jnp.mean(values * values, axis=1, keepdims=True)) + 1e-06)
    scaled = values * inverse
    normed = scaled * norm_gain.astype(jnp.float32)
    activated = jax.nn.gelu(normed, approximate=True).astype(jnp.bfloat16)
    mixed = jnp.dot(activated, proj_weight, preferred_element_type=jnp.float32) + proj_bias.astype(jnp.float32)
    pooled = lax.optimization_barrier(jnp.mean(mixed.reshape(row_count // 2, 2, -1), axis=1)).astype(jnp.bfloat16)
    grad_mixed = (jnp.repeat(cotan.astype(jnp.float32), 2, axis=0) * scale_factor).astype(jnp.bfloat16)
    grad_proj_weight = lax.dot_general(activated, grad_mixed, (((0,), (0,)), ((), ())), preferred_element_type=jnp.float32)
    grad_proj_bias = lax.optimization_barrier(jnp.sum(grad_mixed.astype(jnp.float32), axis=0))
    grad_activated = lax.dot_general(grad_mixed, proj_weight, (((1,), (1,)), ((), ())), preferred_element_type=jnp.float32)
    _, pullback = jax.vjp(lambda v: jax.nn.gelu(v, approximate=True), normed)
    grad_normed = pullback(grad_activated)[0]
    grad_norm_gain = lax.optimization_barrier(jnp.sum(grad_normed * scaled, axis=0))
    weighted = grad_normed * norm_gain.astype(jnp.float32)
    grad_embedded = (inverse * (weighted - scaled * lax.optimization_barrier(jnp.mean(weighted * scaled, axis=1, keepdims=True)))).astype(jnp.bfloat16)
    grad_embed_weight = lax.dot_general(features, grad_embedded, (((0,), (0,)), ((), ())), preferred_element_type=jnp.float32).reshape(kernel_width, 4, -1)
    grad_embed_bias = lax.optimization_barrier(jnp.sum(grad_embedded.astype(jnp.float32), axis=0))
    return (pooled, (grad_embed_weight, grad_embed_bias, grad_norm_gain, grad_proj_weight, grad_proj_bias))

def reference(bases, embed_weight, embed_bias, norm_gain, proj_weight, proj_bias, cotangent):
    half_width = KW // 2
    codes = jnp.pad(bases + 1, ((0, 0), (half_width, half_width))).astype(jnp.int32)
    scale_factor = 0.5 / (BATCH * SEQ)
    initial = (jnp.zeros((KW, 4, D0), jnp.float32), jnp.zeros((D0,), jnp.float32), jnp.zeros((D0,), jnp.float32), jnp.zeros((D0, D1), jnp.float32), jnp.zeros((D1,), jnp.float32))

    def step(carry, inputs):
        pooled, grads = sample_pass(inputs[0], inputs[1], embed_weight, embed_bias, norm_gain, proj_weight, proj_bias, scale_factor)
        return (tuple((c + g for c, g in zip(carry, grads))), pooled)
    totals, pooled = lax.scan(step, initial, (codes, cotangent))
    return (pooled, totals[0], totals[1], totals[2], totals[3], totals[4])
```

```python
import functools

import jax
import jax.numpy as jnp
from jax import lax
from jax.experimental import pallas as pl
from jax.experimental.pallas import tpu as pltpu
from jax.sharding import PartitionSpec as P

F32, BF16 = jnp.float32, jnp.bfloat16
LANES = 128
GELU_A = 0.7978845608028654
GELU_B = 0.044715
EPSILON = 1e-06


def dot(a, b, contract, precision=None):
    return lax.dot_general(a, b, ((contract[:1], contract[1:]), ((), ())), precision=precision, preferred_element_type=F32)


def iota(shape, dim):
    return lax.broadcasted_iota(jnp.int32, shape, dim)


def step_kernel(dims, core_ref, before_ref, bases_ref, after_ref, own_ref, other_ref, cot_ref,
                pooled_ref, mine_ref, theirs_ref,
                w_ref, code_ref, perm_ref, feat_ref, we_ref, wide_ref, emb_ref, ga_ref, s_ref, ge_ref, gew_ref):
    kw, shards, d0, d1, rows, tile, chunk = dims
    half = w_ref.shape[1] // 2
    pairs, pair_tile = rows // 2, tile // 2
    reach = kw // 2
    taps = kw * 4
    core = core_ref[0]
    per = d1 // shards
    block = d0 // shards

    @pl.when(core == 0)
    def _():
        w_ref[:, :half] = own_ref[...]
        w_ref[:, half:] = other_ref[...]

    @pl.when(core != 0)
    def _():
        w_ref[:, :half] = other_ref[...]
        w_ref[:, half:] = own_ref[...]

    code_ref[:, :LANES] = before_ref[...].astype(F32)
    code_ref[:, LANES:LANES + rows] = (bases_ref[...] + 1).astype(F32)
    code_ref[:, LANES + rows:] = after_ref[...].astype(F32)

    wide = w_ref[:, d1:].astype(F32)
    wide_ref[...] = wide
    we_ref[...] = wide.T.astype(BF16)
    gain = we_ref[pl.ds(64 - 8, 8), :].astype(F32)[5:6, :]

    column = iota((LANES, d1), 1)
    owner = (column * 2341) >> 16
    spread = (iota((LANES, d1), 0) == column - owner * per + 64).astype(F32)
    owned = owner[:shards] == iota((shards, d1), 0)
    pieces = wide_ref[pl.ds(0, shards, stride=block), :]
    bias = jnp.sum(jnp.where(owned, dot(pieces.astype(BF16), spread.astype(BF16), (1, 0)), 0.0), axis=0, keepdims=True)

    source, place = iota((tile, tile), 0), iota((tile, tile), 1)
    perm_ref[...] = (source == jnp.where(place < pair_tile, 2 * place, 2 * (place - pair_tile) + 1)).astype(BF16)
    repeat = ((iota((LANES, 16), 0) >> 2) == iota((LANES, 16), 1)).astype(BF16)
    letter = (iota((LANES, tile), 0) & 3) + 1
    line = iota((LANES, tile), 0)
    for t in range(rows // tile):
        window = code_ref[:, t * tile:t * tile + tile + 2 * LANES]
        start = LANES - reach
        shifted = jnp.concatenate([window[:, start + k:start + k + tile] for k in range(kw)] + [jnp.zeros((1, tile), F32)], axis=0)
        spreaded = dot(repeat, shifted.astype(BF16), (1, 0))
        hot = ((spreaded == letter.astype(F32)) & (line < taps)) | (line == taps)
        ordered = dot(hot.astype(F32).astype(BF16), perm_ref[...], (1, 0))
        feat_ref[:, t * tile:(t + 1) * tile] = ordered.astype(BF16)

    for t in range(rows // tile):
        at = t * tile
        emb_ref[at:at + tile, :] = dot(feat_ref[:, at:at + tile], we_ref[...], (0, 0)).astype(BF16)
        half_at = t * pair_tile
        ga_ref[half_at:half_at + pair_tile, :] = dot(cot_ref[half_at:half_at + pair_tile, :], w_ref[:, :d1], (1, 1))

        def side(start, grad):
            values = emb_ref[pl.ds(start, chunk), :].astype(F32)
            inverse = lax.rsqrt(jnp.sum(values * values, axis=1, keepdims=True) * (1.0 / d0) + EPSILON)
            scaled = values * inverse
            normed = scaled * gain
            square = normed * normed
            tanh = jnp.tanh(normed * (GELU_A + (GELU_A * GELU_B) * square))
            gate = 0.5 + 0.5 * tanh
            activated = normed * gate
            slope = gate + (activated * (1.0 - tanh)) * (GELU_A + (3.0 * GELU_A * GELU_B) * square)
            grad_normed = grad * slope
            toward_gain = grad_normed * scaled
            weighted = grad_normed * gain
            shared = jnp.sum(toward_gain * gain, axis=1, keepdims=True) * (1.0 / d0)
            ge_ref[pl.ds(start, chunk), :] = (inverse * (weighted - scaled * shared)).astype(BF16)
            return activated, toward_gain

        def body(i, total):
            first = pl.multiple_of(at + i * chunk, chunk)
            second = pl.multiple_of(at + pair_tile + i * chunk, chunk)
            pair_at = pl.multiple_of(half_at + i * chunk, chunk)
            grad = ga_ref[pl.ds(pair_at, chunk), :]
            act_even, gain_even = side(first, grad)
            act_odd, gain_odd = side(second, grad)
            s_ref[pl.ds(pair_at, chunk), :] = (act_even + act_odd).astype(BF16)
            both = gain_even + gain_odd
            for r in range(0, chunk, 8):
                total = total + both[r:r + 8]
            return total

        start_total = jnp.zeros((8, d0), F32)
        gain_total = lax.fori_loop(0, pair_tile // chunk, body, start_total)
        pooled_ref[half_at:half_at + pair_tile, :] = (
            0.5 * dot(s_ref[half_at:half_at + pair_tile, :], w_ref[:, :d1], (1, 0)) + bias).astype(BF16)
        part = dot(feat_ref[:, at:at + tile], ge_ref[at:at + tile, :], (1, 0))
        is_gain = iota((LANES, d0), 0) == taps + 1
        part = jnp.where(is_gain, jnp.sum(gain_total, axis=0, keepdims=True), part)
        if t == 0:
            gew_ref[...] = part
        else:
            gew_ref[...] += part

    wide_ref[...] = gew_ref[...].T
    sums = 2.0 * jnp.sum(cot_ref[...].astype(F32), axis=0, keepdims=True)
    pieces = dot(jnp.where(owned, sums, 0.0), spread, (1, 1), lax.Precision.HIGHEST)
    wide_ref[pl.ds(0, shards, stride=block), :] = wide_ref[pl.ds(0, shards, stride=block), :] + pieces

    def halves(first_ref, second_ref):
        first_ref[...] = dot(s_ref[...], cot_ref[:, :half], (0, 0)).astype(first_ref.dtype)
        second_ref[:, :d1 - half] = dot(s_ref[...], cot_ref[:, half:], (0, 0)).astype(second_ref.dtype)
        second_ref[:, d1 - half:] = wide_ref[...].astype(second_ref.dtype)

    @pl.when(core == 0)
    def _():
        halves(mine_ref, theirs_ref)

    @pl.when(core != 0)
    def _():
        halves(theirs_ref, mine_ref)


def train_step(core, before, bases, after, own, other, cot, kw, shards):
    d0, half = own.shape
    pairs, d1 = cot.shape
    rows = 2 * pairs
    width = 2 * half
    tile, chunk = 512, 16
    dims = (kw, shards, d0, d1, rows, tile, chunk)
    vmem = pl.BlockSpec(memory_space=pltpu.VMEM)
    return pl.pallas_call(
        functools.partial(step_kernel, dims),
        out_shape=(
            jax.ShapeDtypeStruct((pairs, d1), BF16),
            jax.ShapeDtypeStruct((d0, half), F32),
            jax.ShapeDtypeStruct((d0, half), BF16),
        ),
        in_specs=[pl.BlockSpec(memory_space=pltpu.SMEM)] + [vmem] * 6,
        out_specs=(vmem, vmem, vmem),
        scratch_shapes=[
            pltpu.VMEM((d0, width), BF16),
            pltpu.VMEM((1, rows + 2 * LANES), F32),
            pltpu.VMEM((tile, tile), BF16),
            pltpu.VMEM((LANES, rows), BF16),
            pltpu.VMEM((LANES, d0), BF16),
            pltpu.VMEM((d0, LANES), F32),
            pltpu.VMEM((rows, d0), BF16),
            pltpu.VMEM((pairs, d0), F32),
            pltpu.VMEM((pairs, d0), BF16),
            pltpu.VMEM((rows, d0), BF16),
            pltpu.VMEM((LANES, d0), F32),
        ],
        compiler_params=pltpu.CompilerParams(vmem_limit_bytes=50 << 20),
        name="train_step",
    )(core, before, bases, after, own, other, cot)


def pack_kernel(core_ref, embed_ref, embed_bias_ref, gain_ref, proj_ref, proj_bias_ref, out_ref, rows_ref, block_ref):
    kw, block, d1 = embed_ref.shape[0], proj_ref.shape[0], proj_ref.shape[1]
    copies, _, half = out_ref.shape
    taps, per = kw * 4, proj_bias_ref.shape[1]
    rows_ref[...] = jnp.zeros_like(rows_ref)
    for k in range(kw):
        rows_ref[4 * k:4 * k + 4, :block] = embed_ref[k].astype(F32)
    rows_ref[taps:taps + 1, :block] = embed_bias_ref[...].astype(F32)
    rows_ref[taps + 1:taps + 2, :block] = gain_ref[...].astype(F32)
    block_ref[...] = rows_ref[...].T[:block]
    block_ref[:1, 64:64 + per] = proj_bias_ref[...].astype(F32)
    edge = d1 - half

    @pl.when(core_ref[0] == 0)
    def _():
        for i in range(copies):
            out_ref[i] = proj_ref[:, :half]

    @pl.when(core_ref[0] != 0)
    def _():
        for i in range(copies):
            out_ref[i, :, :edge] = proj_ref[:, half:]
            out_ref[i, :, edge:] = block_ref[...].astype(BF16)


def sum_kernel(scale, in_ref, out_ref):
    total = in_ref[0].astype(F32)
    for i in range(1, in_ref.shape[0]):
        total = total + in_ref[i].astype(F32)
    if scale != 1.0:
        total = total * scale
    total = total.astype(out_ref.dtype)
    for i in range(out_ref.shape[0]):
        out_ref[i] = total


def unpack_kernel(core_ref, total_ref, across_ref, embed_ref, embed_bias_ref, gain_ref, proj_ref, proj_bias_ref, rows_ref):
    kw, block, d1 = embed_ref.shape[0], proj_ref.shape[0], proj_ref.shape[1]
    half = total_ref.shape[1]
    taps, per, edge = kw * 4, proj_bias_ref.shape[1], d1 - half

    def place(left_ref, right_ref):
        proj_ref[:, :half] = left_ref[...]
        proj_ref[:, half:] = right_ref[:, :edge]
        rows_ref[:block, :] = right_ref[:, edge:]

    @pl.when(core_ref[0] == 0)
    def _():
        place(total_ref, across_ref)

    @pl.when(core_ref[0] != 0)
    def _():
        place(across_ref, total_ref)

    proj_bias_ref[...] = rows_ref[:1, 64:64 + per]
    rows_ref[block:, :] = jnp.zeros((LANES - block, LANES), F32)
    rows_ref[...] = rows_ref[...].T
    for k in range(kw):
        embed_ref[k] = rows_ref[4 * k:4 * k + 4, :block]
    embed_bias_ref[...] = rows_ref[taps:taps + 1, :block]
    gain_ref[...] = rows_ref[taps + 1:taps + 2, :block]


VMEM = pl.BlockSpec(memory_space=pltpu.VMEM)
SMEM = pl.BlockSpec(memory_space=pltpu.SMEM)


def local(bases, embed_weight, embed_bias, norm_gain, proj_weight, proj_bias, cotangent):
    kw = embed_weight.shape[0]
    shards, members = lax.axis_size("dp"), lax.axis_size("seq")
    block, d1 = proj_weight.shape
    per = proj_bias.shape[0]
    half = (d1 + LANES) // 2
    core = (lax.axis_index("seq") & 1).astype(jnp.int32).reshape(1)
    swap = [(i, i ^ 1) for i in range(members)]

    codes = bases + 1
    before = lax.ppermute(codes[:, -LANES:], "seq", [(i, i + 1) for i in range(members - 1)])
    after = lax.ppermute(codes[:, :LANES], "seq", [(i + 1, i) for i in range(members - 1)])

    piece = pl.pallas_call(
        pack_kernel,
        out_shape=jax.ShapeDtypeStruct((shards, block, half), BF16),
        in_specs=[SMEM] + [VMEM] * 5,
        out_specs=VMEM,
        scratch_shapes=[pltpu.VMEM((LANES, LANES), F32), pltpu.VMEM((block, LANES), F32)],
        name="pack",
    )(core, embed_weight, embed_bias[None], norm_gain[None], proj_weight, proj_bias[None])
    own = lax.all_to_all(piece, "dp", 0, 0, tiled=True).reshape(shards * block, half)
    other = lax.ppermute(own, "seq", swap)

    pooled, mine, theirs = train_step(core, before, bases, after, own, other, cotangent[0], kw, shards)

    came = lax.ppermute(theirs, "seq", swap)
    summed = (mine + came.astype(F32)).astype(BF16).reshape(shards, block, half)
    parts = lax.all_to_all(summed, "dp", 0, 0, tiled=True)

    def add_up(parts, scale, copies, kind):
        return pl.pallas_call(
            functools.partial(sum_kernel, scale),
            out_shape=jax.ShapeDtypeStruct((copies, block, half), kind),
            in_specs=[VMEM],
            out_specs=VMEM,
            name="add_up",
        )(parts)

    groups = [[i for i in range(members) if i % 2 == c] for c in range(2)]
    spread = lax.all_to_all(add_up(parts, 1.0, members // 2, BF16), "seq", 0, 0, axis_index_groups=groups, tiled=True)
    total = add_up(spread, 0.25 / (cotangent.shape[1] * members * shards), 1, F32)[0]
    across = lax.ppermute(total, "seq", swap)
    grad_embed, grad_embed_bias, grad_gain, grad_proj, grad_proj_bias = pl.pallas_call(
        unpack_kernel,
        out_shape=(
            jax.ShapeDtypeStruct(embed_weight.shape, F32),
            jax.ShapeDtypeStruct((1, block), F32),
            jax.ShapeDtypeStruct((1, block), F32),
            jax.ShapeDtypeStruct((block, d1), F32),
            jax.ShapeDtypeStruct((1, per), F32),
        ),
        in_specs=[SMEM, VMEM, VMEM],
        out_specs=(VMEM,) * 5,
        scratch_shapes=[pltpu.VMEM((LANES, LANES), F32)],
        name="unpack",
    )(core, total, across)
    return (pooled[None], grad_embed, grad_embed_bias[0], grad_gain[0], grad_proj, grad_proj_bias[0])


def solution(mesh):
    placed = (
        P("dp", "seq"),
        P(None, None, "dp"),
        P("dp"),
        P("dp"),
        P("dp", None),
        P("dp"),
        P("dp", "seq", None),
    )
    return jax.shard_map(
        local,
        mesh=mesh,
        in_specs=placed,
        out_specs=(
            P("dp", "seq", None),
            P(None, None, "dp"),
            P("dp"),
            P("dp"),
            P("dp", None),
            P("dp"),
        ),
        check_vma=False,
    )
```

```python
import functools

import jax
import jax.numpy as jnp
from jax import lax
from jax.experimental import pallas as pl
from jax.experimental.pallas import tpu as pltpu
from jax.sharding import PartitionSpec as P

F32, BF16 = jnp.float32, jnp.bfloat16
LANES = 128
GELU_A = 0.7978845608028654
GELU_B = 0.044715
GELU_K = (GELU_A * GELU_B) ** (1 / 3)
GELU_C = GELU_A / GELU_K
EPSILON = 1e-06


def dot(a, b, contract, precision=None):
    return lax.dot_general(a, b, ((contract[:1], contract[1:]), ((), ())), precision=precision, preferred_element_type=F32)


def iota(shape, dim):
    return lax.broadcasted_iota(jnp.int32, shape, dim)


def step_kernel(dims, core_ref, before_ref, bases_ref, after_ref, own_ref, other_ref, cot_ref,
                pooled_ref, mine_ref, theirs_ref,
                w_ref, code_ref, perm_ref, feat_ref, we_ref, wide_ref, emb_ref, ga_ref, s_ref, ge_ref, gew_ref):
    kw, shards, d0, d1, rows, tile, chunk = dims
    half = w_ref.shape[1] // 2
    pairs, pair_tile = rows // 2, tile // 2
    reach = kw // 2
    taps = kw * 4
    core = core_ref[0]
    per = d1 // shards
    block = d0 // shards

    @pl.when(core == 0)
    def _():
        w_ref[:, :half] = own_ref[...]
        w_ref[:, half:] = other_ref[...]

    @pl.when(core != 0)
    def _():
        w_ref[:, :half] = other_ref[...]
        w_ref[:, half:] = own_ref[...]

    code_ref[:, :LANES] = before_ref[...].astype(F32)
    code_ref[:, LANES:LANES + rows] = (bases_ref[...] + 1).astype(F32)
    code_ref[:, LANES + rows:] = after_ref[...].astype(F32)

    wide = w_ref[:, d1:].astype(F32)
    wide_ref[...] = wide
    we_ref[...] = wide.T.astype(BF16)
    gain = we_ref[pl.ds(64 - 8, 8), :].astype(F32)[5:6, :]
    gain_y = gain * GELU_K

    column = iota((LANES, d1), 1)
    owner = (column * 2341) >> 16
    spread = (iota((LANES, d1), 0) == column - owner * per + 64).astype(F32)
    owned = owner[:shards] == iota((shards, d1), 0)
    pieces = wide_ref[pl.ds(0, shards, stride=block), :]
    bias = jnp.sum(jnp.where(owned, dot(pieces.astype(BF16), spread.astype(BF16), (1, 0)), 0.0), axis=0, keepdims=True)

    source, place = iota((tile, tile), 0), iota((tile, tile), 1)
    perm_ref[...] = (source == jnp.where(place < pair_tile, 2 * place, 2 * (place - pair_tile) + 1)).astype(BF16)
    repeat = ((iota((LANES, 16), 0) >> 2) == iota((LANES, 16), 1)).astype(BF16)
    letter = (iota((LANES, tile), 0) & 3) + 1
    line = iota((LANES, tile), 0)
    for t in range(rows // tile):
        window = code_ref[:, t * tile:t * tile + tile + 2 * LANES]
        start = LANES - reach
        shifted = jnp.concatenate([window[:, start + k:start + k + tile] for k in range(kw)] + [jnp.zeros((1, tile), F32)], axis=0)
        spreaded = dot(repeat, shifted.astype(BF16), (1, 0))
        hot = ((spreaded == letter.astype(F32)) & (line < taps)) | (line == taps)
        ordered = dot(hot.astype(F32).astype(BF16), perm_ref[...], (1, 0))
        feat_ref[:, t * tile:(t + 1) * tile] = ordered.astype(BF16)

    for t in range(rows // tile):
        at = t * tile
        emb_ref[at:at + tile, :] = dot(feat_ref[:, at:at + tile], we_ref[...], (0, 0)).astype(BF16)
        half_at = t * pair_tile
        ga_ref[half_at:half_at + pair_tile, :] = dot(cot_ref[half_at:half_at + pair_tile, :], w_ref[:, :d1], (1, 1))

        def side(start, grad):
            values = emb_ref[pl.ds(start, chunk), :].astype(F32)
            inverse = lax.rsqrt(jnp.sum(values * values, axis=1, keepdims=True) * (1.0 / d0) + EPSILON)
            y = (values * inverse) * gain_y
            square = y * y
            tanh = jnp.tanh(y * (GELU_C + square))
            above, below = 1.0 + tanh, 1.0 - tanh
            activated = y * above
            slope = above + (activated * below) * (GELU_C + 3.0 * square)
            grad_normed = grad * slope
            toward_gain = grad_normed * y
            shared = jnp.sum(toward_gain, axis=1, keepdims=True) * (inverse * inverse * (1.0 / (GELU_K * d0)))
            ge_ref[pl.ds(start, chunk), :] = (inverse * (grad_normed * gain) - values * shared).astype(BF16)
            return activated, toward_gain

        def body(i, total):
            first = pl.multiple_of(at + i * chunk, chunk)
            second = pl.multiple_of(at + pair_tile + i * chunk, chunk)
            pair_at = pl.multiple_of(half_at + i * chunk, chunk)
            grad = ga_ref[pl.ds(pair_at, chunk), :]
            act_even, gain_even = side(first, grad)
            act_odd, gain_odd = side(second, grad)
            s_ref[pl.ds(pair_at, chunk), :] = (act_even + act_odd).astype(BF16)
            both = gain_even + gain_odd
            for r in range(0, chunk, 8):
                total = total + both[r:r + 8]
            return total

        start_total = jnp.zeros((8, d0), F32)
        gain_total = lax.fori_loop(0, pair_tile // chunk, body, start_total, unroll=True)
        pooled_ref[half_at:half_at + pair_tile, :] = (
            (0.25 / GELU_K) * dot(s_ref[half_at:half_at + pair_tile, :], w_ref[:, :d1], (1, 0)) + bias).astype(BF16)
        part = dot(feat_ref[:, at:at + tile], ge_ref[at:at + tile, :], (1, 0))
        is_gain = iota((LANES, d0), 0) == taps + 1
        part = jnp.where(is_gain, jnp.sum(gain_total, axis=0, keepdims=True) / gain_y, part)
        if t == 0:
            gew_ref[...] = part
        else:
            gew_ref[...] += part

    wide_ref[...] = gew_ref[...].T
    sums = 4.0 * jnp.sum(cot_ref[...].astype(F32), axis=0, keepdims=True)
    pieces = dot(jnp.where(owned, sums, 0.0), spread, (1, 1), lax.Precision.HIGHEST)
    wide_ref[pl.ds(0, shards, stride=block), :] = wide_ref[pl.ds(0, shards, stride=block), :] + pieces

    def halves(first_ref, second_ref):
        first_ref[...] = (dot(s_ref[...], cot_ref[:, :half], (0, 0)) * (1.0 / GELU_K)).astype(first_ref.dtype)
        second_ref[:, :d1 - half] = (dot(s_ref[...], cot_ref[:, half:], (0, 0)) * (1.0 / GELU_K)).astype(second_ref.dtype)
        second_ref[:, d1 - half:] = wide_ref[...].astype(second_ref.dtype)

    @pl.when(core == 0)
    def _():
        halves(mine_ref, theirs_ref)

    @pl.when(core != 0)
    def _():
        halves(theirs_ref, mine_ref)


def train_step(core, before, bases, after, own, other, cot, kw, shards):
    d0, half = own.shape
    pairs, d1 = cot.shape
    rows = 2 * pairs
    width = 2 * half
    tile, chunk = 512, 32
    dims = (kw, shards, d0, d1, rows, tile, chunk)
    vmem = pl.BlockSpec(memory_space=pltpu.VMEM)
    return pl.pallas_call(
        functools.partial(step_kernel, dims),
        out_shape=(
            jax.ShapeDtypeStruct((pairs, d1), BF16),
            jax.ShapeDtypeStruct((d0, half), F32),
            jax.ShapeDtypeStruct((d0, half), BF16),
        ),
        in_specs=[pl.BlockSpec(memory_space=pltpu.SMEM)] + [vmem] * 6,
        out_specs=(vmem, vmem, vmem),
        scratch_shapes=[
            pltpu.VMEM((d0, width), BF16),
            pltpu.VMEM((1, rows + 2 * LANES), F32),
            pltpu.VMEM((tile, tile), BF16),
            pltpu.VMEM((LANES, rows), BF16),
            pltpu.VMEM((LANES, d0), BF16),
            pltpu.VMEM((d0, LANES), F32),
            pltpu.VMEM((rows, d0), BF16),
            pltpu.VMEM((pairs, d0), F32),
            pltpu.VMEM((pairs, d0), BF16),
            pltpu.VMEM((rows, d0), BF16),
            pltpu.VMEM((LANES, d0), F32),
        ],
        compiler_params=pltpu.CompilerParams(vmem_limit_bytes=28 << 20),
        name="train_step",
    )(core, before, bases, after, own, other, cot)


def pack_kernel(core_ref, embed_ref, embed_bias_ref, gain_ref, proj_ref, proj_bias_ref, out_ref, rows_ref, block_ref):
    kw, block, d1 = embed_ref.shape[0], proj_ref.shape[0], proj_ref.shape[1]
    copies, _, half = out_ref.shape
    taps, per = kw * 4, proj_bias_ref.shape[1]
    rows_ref[...] = jnp.zeros_like(rows_ref)
    for k in range(kw):
        rows_ref[4 * k:4 * k + 4, :block] = embed_ref[k].astype(F32)
    rows_ref[taps:taps + 1, :block] = embed_bias_ref[...].astype(F32)
    rows_ref[taps + 1:taps + 2, :block] = gain_ref[...].astype(F32)
    block_ref[...] = rows_ref[...].T[:block]
    block_ref[:1, 64:64 + per] = proj_bias_ref[...].astype(F32)
    edge = d1 - half

    @pl.when(core_ref[0] == 0)
    def _():
        for i in range(copies):
            out_ref[i] = proj_ref[:, :half]

    @pl.when(core_ref[0] != 0)
    def _():
        for i in range(copies):
            out_ref[i, :, :edge] = proj_ref[:, half:]
            out_ref[i, :, edge:] = block_ref[...].astype(BF16)


def sum_kernel(scale, in_ref, out_ref):
    total = in_ref[0].astype(F32)
    for i in range(1, in_ref.shape[0]):
        total = total + in_ref[i].astype(F32)
    if scale != 1.0:
        total = total * scale
    total = total.astype(out_ref.dtype)
    for i in range(out_ref.shape[0]):
        out_ref[i] = total


def unpack_kernel(core_ref, total_ref, across_ref, embed_ref, embed_bias_ref, gain_ref, proj_ref, proj_bias_ref, rows_ref):
    kw, block, d1 = embed_ref.shape[0], proj_ref.shape[0], proj_ref.shape[1]
    half = total_ref.shape[1]
    taps, per, edge = kw * 4, proj_bias_ref.shape[1], d1 - half

    def place(left_ref, right_ref):
        proj_ref[:, :half] = left_ref[...]
        proj_ref[:, half:] = right_ref[:, :edge]
        rows_ref[:block, :] = right_ref[:, edge:]

    @pl.when(core_ref[0] == 0)
    def _():
        place(total_ref, across_ref)

    @pl.when(core_ref[0] != 0)
    def _():
        place(across_ref, total_ref)

    proj_bias_ref[...] = rows_ref[:1, 64:64 + per]
    rows_ref[block:, :] = jnp.zeros((LANES - block, LANES), F32)
    rows_ref[...] = rows_ref[...].T
    for k in range(kw):
        embed_ref[k] = rows_ref[4 * k:4 * k + 4, :block]
    embed_bias_ref[...] = rows_ref[taps:taps + 1, :block]
    gain_ref[...] = rows_ref[taps + 1:taps + 2, :block]


VMEM = pl.BlockSpec(memory_space=pltpu.VMEM)
SMEM = pl.BlockSpec(memory_space=pltpu.SMEM)


def local(bases, embed_weight, embed_bias, norm_gain, proj_weight, proj_bias, cotangent):
    kw = embed_weight.shape[0]
    shards, members = lax.axis_size("dp"), lax.axis_size("seq")
    block, d1 = proj_weight.shape
    per = proj_bias.shape[0]
    half = (d1 + LANES) // 2
    core = (lax.axis_index("seq") & 1).astype(jnp.int32).reshape(1)
    swap = [(i, i ^ 1) for i in range(members)]

    codes = bases + 1
    before = lax.ppermute(codes[:, -LANES:], "seq", [(i, i + 1) for i in range(members - 1)])
    after = lax.ppermute(codes[:, :LANES], "seq", [(i + 1, i) for i in range(members - 1)])

    piece = pl.pallas_call(
        pack_kernel,
        out_shape=jax.ShapeDtypeStruct((shards, block, half), BF16),
        in_specs=[SMEM] + [VMEM] * 5,
        out_specs=VMEM,
        scratch_shapes=[pltpu.VMEM((LANES, LANES), F32), pltpu.VMEM((block, LANES), F32)],
        compiler_params=pltpu.CompilerParams(vmem_limit_bytes=4 << 20),
        name="pack",
    )(core, embed_weight, embed_bias[None], norm_gain[None], proj_weight, proj_bias[None])
    own = lax.all_to_all(piece, "dp", 0, 0, tiled=True).reshape(shards * block, half)
    other = lax.ppermute(own, "seq", swap)

    pooled, mine, theirs = train_step(core, before, bases, after, own, other, cotangent[0], kw, shards)

    came = lax.ppermute(theirs, "seq", swap)
    summed = (mine + came.astype(F32)).astype(BF16).reshape(shards, block, half)
    parts = lax.all_to_all(summed, "dp", 0, 0, tiled=True)

    def add_up(parts, scale, copies, kind):
        return pl.pallas_call(
            functools.partial(sum_kernel, scale),
            out_shape=jax.ShapeDtypeStruct((copies, block, half), kind),
            in_specs=[VMEM],
            out_specs=VMEM,
            compiler_params=pltpu.CompilerParams(vmem_limit_bytes=4 << 20),
            name="add_up",
        )(parts)

    groups = [[i for i in range(members) if i % 2 == c] for c in range(2)]
    spread = lax.all_to_all(add_up(parts, 1.0, members // 2, BF16), "seq", 0, 0, axis_index_groups=groups, tiled=True)
    total = add_up(spread, 0.125 / (cotangent.shape[1] * members * shards), 1, F32)[0]
    across = lax.ppermute(total, "seq", swap)
    grad_embed, grad_embed_bias, grad_gain, grad_proj, grad_proj_bias = pl.pallas_call(
        unpack_kernel,
        out_shape=(
            jax.ShapeDtypeStruct(embed_weight.shape, F32),
            jax.ShapeDtypeStruct((1, block), F32),
            jax.ShapeDtypeStruct((1, block), F32),
            jax.ShapeDtypeStruct((block, d1), F32),
            jax.ShapeDtypeStruct((1, per), F32),
        ),
        in_specs=[SMEM, VMEM, VMEM],
        out_specs=(VMEM,) * 5,
        scratch_shapes=[pltpu.VMEM((LANES, LANES), F32)],
        compiler_params=pltpu.CompilerParams(vmem_limit_bytes=4 << 20),
        name="unpack",
    )(core, total, across)
    return (pooled[None], grad_embed, grad_embed_bias[0], grad_gain[0], grad_proj, grad_proj_bias[0])


def solution(mesh):
    placed = (
        P("dp", "seq"),
        P(None, None, "dp"),
        P("dp"),
        P("dp"),
        P("dp", None),
        P("dp"),
        P("dp", "seq", None),
    )
    return jax.shard_map(
        local,
        mesh=mesh,
        in_specs=placed,
        out_specs=(
            P("dp", "seq", None),
            P(None, None, "dp"),
            P("dp"),
            P("dp"),
            P("dp", None),
            P("dp"),
        ),
        check_vma=False,
    )
```

```python
import functools

import jax
import jax.numpy as jnp
from jax import lax
from jax.experimental import pallas as pl
from jax.experimental.pallas import tpu as pltpu
from jax.sharding import PartitionSpec as P

F32, BF16 = jnp.float32, jnp.bfloat16
LANES = 128
GELU_A = 0.7978845608028654
GELU_B = 0.044715
GELU_K = (GELU_A * GELU_B) ** (1 / 3)
GELU_C = GELU_A / GELU_K
EPSILON = 1e-06


def dot(a, b, contract, precision=None):
    return lax.dot_general(a, b, ((contract[:1], contract[1:]), ((), ())), precision=precision, preferred_element_type=F32)


def iota(shape, dim):
    return lax.broadcasted_iota(jnp.int32, shape, dim)


def step_kernel(dims, core_ref, inner_ref, bases_ref, outer_ref, own_ref, other_ref, cot_ref,
                pooled_ref, mine_ref, theirs_ref,
                w_ref, code_ref, perm_ref, feat_ref, we_ref, wide_ref, emb_ref, ga_ref, s_ref, ge_ref, gew_ref):
    kw, shards, d0, d1, rows, tile, chunk = dims
    half = w_ref.shape[1] // 2
    pairs, pair_tile = rows // 2, tile // 2
    reach = kw // 2
    taps = kw * 4
    core = core_ref[0]
    per = d1 // shards
    block = d0 // shards

    @pl.when(core == 0)
    def _():
        w_ref[:, :half] = own_ref[...]
        w_ref[:, half:] = other_ref[...]
        code_ref[:, :LANES] = outer_ref[...].astype(F32)
        code_ref[:, LANES + rows:] = inner_ref[...].astype(F32)

    @pl.when(core != 0)
    def _():
        w_ref[:, :half] = other_ref[...]
        w_ref[:, half:] = own_ref[...]
        code_ref[:, :LANES] = inner_ref[...].astype(F32)
        code_ref[:, LANES + rows:] = outer_ref[...].astype(F32)

    code_ref[:, LANES:LANES + rows] = (bases_ref[...] + 1).astype(F32)

    wide = w_ref[:, d1:].astype(F32)
    wide_ref[...] = wide
    we_ref[...] = wide.T.astype(BF16)
    gain = we_ref[pl.ds(64 - 8, 8), :].astype(F32)[5:6, :]
    gain_y = gain * GELU_K

    column = iota((LANES, d1), 1)
    owner = (column * 2341) >> 16
    spread = (iota((LANES, d1), 0) == column - owner * per + 64).astype(F32)
    owned = owner[:shards] == iota((shards, d1), 0)
    pieces = wide_ref[pl.ds(0, shards, stride=block), :]
    bias = jnp.sum(jnp.where(owned, dot(pieces.astype(BF16), spread.astype(BF16), (1, 0)), 0.0), axis=0, keepdims=True)

    source, place = iota((tile, tile), 0), iota((tile, tile), 1)
    perm_ref[...] = (source == jnp.where(place < pair_tile, 2 * place, 2 * (place - pair_tile) + 1)).astype(BF16)
    repeat = ((iota((LANES, 16), 0) >> 2) == iota((LANES, 16), 1)).astype(BF16)
    letter = (iota((LANES, tile), 0) & 3) + 1
    line = iota((LANES, tile), 0)
    for t in range(rows // tile):
        window = code_ref[:, t * tile:t * tile + tile + 2 * LANES]
        start = LANES - reach
        shifted = jnp.concatenate([window[:, start + k:start + k + tile] for k in range(kw)] + [jnp.zeros((1, tile), F32)], axis=0)
        spreaded = dot(repeat, shifted.astype(BF16), (1, 0))
        hot = ((spreaded == letter.astype(F32)) & (line < taps)) | (line == taps)
        ordered = dot(hot.astype(F32).astype(BF16), perm_ref[...], (1, 0))
        feat_ref[:, t * tile:(t + 1) * tile] = ordered.astype(BF16)

    for t in range(rows // tile):
        at = t * tile
        emb_ref[at:at + tile, :] = dot(feat_ref[:, at:at + tile], we_ref[...], (0, 0)).astype(BF16)
        half_at = t * pair_tile
        ga_ref[half_at:half_at + pair_tile, :] = dot(cot_ref[half_at:half_at + pair_tile, :], w_ref[:, :d1], (1, 1))

        def side(start, grad):
            values = emb_ref[pl.ds(start, chunk), :].astype(F32)
            inverse = lax.rsqrt(jnp.sum(values * values, axis=1, keepdims=True) * (1.0 / d0) + EPSILON)
            y = (values * inverse) * gain_y
            square = y * y
            tanh = jnp.tanh(y * (GELU_C + square))
            above, below = 1.0 + tanh, 1.0 - tanh
            activated = y * above
            slope = above + (activated * below) * (GELU_C + 3.0 * square)
            grad_normed = grad * slope
            toward_gain = grad_normed * y
            shared = jnp.sum(toward_gain, axis=1, keepdims=True) * (inverse * inverse * (1.0 / (GELU_K * d0)))
            ge_ref[pl.ds(start, chunk), :] = (inverse * (grad_normed * gain) - values * shared).astype(BF16)
            return activated, toward_gain

        def body(i, total):
            first = pl.multiple_of(at + i * chunk, chunk)
            second = pl.multiple_of(at + pair_tile + i * chunk, chunk)
            pair_at = pl.multiple_of(half_at + i * chunk, chunk)
            grad = ga_ref[pl.ds(pair_at, chunk), :]
            act_even, gain_even = side(first, grad)
            act_odd, gain_odd = side(second, grad)
            s_ref[pl.ds(pair_at, chunk), :] = (act_even + act_odd).astype(BF16)
            both = gain_even + gain_odd
            for r in range(0, chunk, 8):
                total = total + both[r:r + 8]
            return total

        start_total = jnp.zeros((8, d0), F32)
        gain_total = lax.fori_loop(0, pair_tile // chunk, body, start_total, unroll=True)
        pooled_ref[half_at:half_at + pair_tile, :] = (
            (0.25 / GELU_K) * dot(s_ref[half_at:half_at + pair_tile, :], w_ref[:, :d1], (1, 0)) + bias).astype(BF16)
        part = dot(feat_ref[:, at:at + tile], ge_ref[at:at + tile, :], (1, 0))
        is_gain = iota((LANES, d0), 0) == taps + 1
        part = jnp.where(is_gain, jnp.sum(gain_total, axis=0, keepdims=True) / gain_y, part)
        if t == 0:
            gew_ref[...] = part
        else:
            gew_ref[...] += part

    wide_ref[...] = gew_ref[...].T
    sums = 4.0 * jnp.sum(cot_ref[...].astype(F32), axis=0, keepdims=True)
    pieces = dot(jnp.where(owned, sums, 0.0), spread, (1, 1), lax.Precision.HIGHEST)
    wide_ref[pl.ds(0, shards, stride=block), :] = wide_ref[pl.ds(0, shards, stride=block), :] + pieces

    def halves(first_ref, second_ref):
        first_ref[...] = (dot(s_ref[...], cot_ref[:, :half], (0, 0)) * (1.0 / GELU_K)).astype(first_ref.dtype)
        second_ref[:, :d1 - half] = (dot(s_ref[...], cot_ref[:, half:], (0, 0)) * (1.0 / GELU_K)).astype(second_ref.dtype)
        second_ref[:, d1 - half:] = wide_ref[...].astype(second_ref.dtype)

    @pl.when(core == 0)
    def _():
        halves(mine_ref, theirs_ref)

    @pl.when(core != 0)
    def _():
        halves(theirs_ref, mine_ref)


def train_step(core, inner, bases, outer, own, other, cot, kw, shards):
    d0, half = own.shape
    pairs, d1 = cot.shape
    rows = 2 * pairs
    width = 2 * half
    tile, chunk = 512, 32
    dims = (kw, shards, d0, d1, rows, tile, chunk)
    vmem = pl.BlockSpec(memory_space=pltpu.VMEM)
    return pl.pallas_call(
        functools.partial(step_kernel, dims),
        out_shape=(
            jax.ShapeDtypeStruct((pairs, d1), BF16),
            jax.ShapeDtypeStruct((d0, half), F32),
            jax.ShapeDtypeStruct((d0, half), BF16),
        ),
        in_specs=[pl.BlockSpec(memory_space=pltpu.SMEM)] + [vmem] * 6,
        out_specs=(vmem, vmem, vmem),
        scratch_shapes=[
            pltpu.VMEM((d0, width), BF16),
            pltpu.VMEM((1, rows + 2 * LANES), F32),
            pltpu.VMEM((tile, tile), BF16),
            pltpu.VMEM((LANES, rows), BF16),
            pltpu.VMEM((LANES, d0), BF16),
            pltpu.VMEM((d0, LANES), F32),
            pltpu.VMEM((rows, d0), BF16),
            pltpu.VMEM((pairs, d0), F32),
            pltpu.VMEM((pairs, d0), BF16),
            pltpu.VMEM((rows, d0), BF16),
            pltpu.VMEM((LANES, d0), F32),
        ],
        compiler_params=pltpu.CompilerParams(vmem_limit_bytes=28 << 20),
        name="train_step",
    )(core, inner, bases, outer, own, other, cot)


def pack_kernel(core_ref, bases_hbm, embed_hbm, embed_bias_hbm, gain_hbm, proj_hbm, proj_bias_hbm,
                out_ref, inner_ref, outer_ref,
                bases_ref, embed_ref, embed_bias_ref, gain_ref, proj_ref, proj_bias_ref, rows_ref, block_ref, sems):
    kw, block, d1 = embed_ref.shape[0], proj_ref.shape[0], proj_ref.shape[1]
    copies, _, half = out_ref.shape
    taps, per = kw * 4, proj_bias_ref.shape[1]
    fetched = [
        pltpu.make_async_copy(source, target, sems.at[n])
        for n, (source, target) in enumerate((
            (bases_hbm, bases_ref), (embed_hbm, embed_ref), (embed_bias_hbm, embed_bias_ref),
            (gain_hbm, gain_ref), (proj_hbm, proj_ref), (proj_bias_hbm, proj_bias_ref)))
    ]
    for copy in fetched:
        copy.start()
    rows_ref[...] = jnp.zeros_like(rows_ref)
    for copy in fetched:
        copy.wait()
    first = bases_ref[:, :LANES] + 1
    last = bases_ref[:, bases_ref.shape[1] - LANES:] + 1
    even = core_ref[0] == 0
    inner_ref[...] = jnp.where(even, last, first)
    outer_ref[...] = jnp.where(even, first, last)
    for k in range(kw):
        rows_ref[4 * k:4 * k + 4, :block] = embed_ref[k].astype(F32)
    rows_ref[taps:taps + 1, :block] = embed_bias_ref[...].astype(F32)
    rows_ref[taps + 1:taps + 2, :block] = gain_ref[...].astype(F32)
    block_ref[...] = rows_ref[...].T[:block]
    block_ref[:1, 64:64 + per] = proj_bias_ref[...].astype(F32)
    edge = d1 - half

    @pl.when(even)
    def _():
        for i in range(copies):
            out_ref[i] = proj_ref[:, :half]

    @pl.when(jnp.logical_not(even))
    def _():
        for i in range(copies):
            out_ref[i, :, :edge] = proj_ref[:, half:]
            out_ref[i, :, edge:] = block_ref[...].astype(BF16)


def sum_kernel(scale, in_ref, out_ref):
    total = in_ref[0].astype(F32)
    for i in range(1, in_ref.shape[0]):
        total = total + in_ref[i].astype(F32)
    if scale != 1.0:
        total = total * scale
    total = total.astype(out_ref.dtype)
    for i in range(out_ref.shape[0]):
        out_ref[i] = total


def unpack_kernel(core_ref, total_ref, across_ref, embed_ref, embed_bias_ref, gain_ref, proj_ref, proj_bias_ref, rows_ref):
    kw, block, d1 = embed_ref.shape[0], proj_ref.shape[0], proj_ref.shape[1]
    half = total_ref.shape[1]
    taps, per, edge = kw * 4, proj_bias_ref.shape[1], d1 - half

    def place(left_ref, right_ref):
        proj_ref[:, :half] = left_ref[...]
        proj_ref[:, half:] = right_ref[:, :edge]
        rows_ref[:block, :] = right_ref[:, edge:]

    @pl.when(core_ref[0] == 0)
    def _():
        place(total_ref, across_ref)

    @pl.when(core_ref[0] != 0)
    def _():
        place(across_ref, total_ref)

    proj_bias_ref[...] = rows_ref[:1, 64:64 + per]
    rows_ref[block:, :] = jnp.zeros((LANES - block, LANES), F32)
    rows_ref[...] = rows_ref[...].T
    for k in range(kw):
        embed_ref[k] = rows_ref[4 * k:4 * k + 4, :block]
    embed_bias_ref[...] = rows_ref[taps:taps + 1, :block]
    gain_ref[...] = rows_ref[taps + 1:taps + 2, :block]


VMEM = pl.BlockSpec(memory_space=pltpu.VMEM)
SMEM = pl.BlockSpec(memory_space=pltpu.SMEM)


def local(bases, embed_weight, embed_bias, norm_gain, proj_weight, proj_bias, cotangent):
    kw = embed_weight.shape[0]
    shards, members = lax.axis_size("dp"), lax.axis_size("seq")
    block, d1 = proj_weight.shape
    per = proj_bias.shape[0]
    half = (d1 + LANES) // 2
    core = (lax.axis_index("seq") & 1).astype(jnp.int32).reshape(1)
    swap = [(i, i ^ 1) for i in range(members)]

    facing = [(i, i + 1 if i % 2 else i - 1) for i in range(1, members - 1)]

    hbm = pl.BlockSpec(memory_space=pltpu.HBM)
    gathered = (bases, embed_weight, embed_bias[None], norm_gain[None], proj_weight, proj_bias[None])
    piece, inner, outer = pl.pallas_call(
        pack_kernel,
        out_shape=(
            jax.ShapeDtypeStruct((shards, block, half), BF16),
            jax.ShapeDtypeStruct((1, LANES), jnp.int32),
            jax.ShapeDtypeStruct((1, LANES), jnp.int32),
        ),
        in_specs=[SMEM] + [hbm] * 6,
        out_specs=(VMEM,) * 3,
        scratch_shapes=[pltpu.VMEM(x.shape, x.dtype) for x in gathered] + [
            pltpu.VMEM((LANES, LANES), F32), pltpu.VMEM((block, LANES), F32), pltpu.SemaphoreType.DMA((6,))],
        compiler_params=pltpu.CompilerParams(vmem_limit_bytes=60 << 20),
        name="pack",
    )(core, *gathered)
    inner = lax.ppermute(inner, "seq", swap)
    outer = lax.ppermute(outer, "seq", facing)
    own = lax.all_to_all(piece, "dp", 0, 0, tiled=True).reshape(shards * block, half)
    other = lax.ppermute(own, "seq", swap)

    pooled, mine, theirs = train_step(core, inner, bases, outer, own, other, cotangent[0], kw, shards)

    came = lax.ppermute(theirs, "seq", swap)
    summed = (mine + came.astype(F32)).astype(BF16).reshape(shards, block, half)
    parts = lax.all_to_all(summed, "dp", 0, 0, tiled=True)

    def add_up(parts, scale, copies, kind):
        return pl.pallas_call(
            functools.partial(sum_kernel, scale),
            out_shape=jax.ShapeDtypeStruct((copies, block, half), kind),
            in_specs=[VMEM],
            out_specs=VMEM,
            compiler_params=pltpu.CompilerParams(vmem_limit_bytes=4 << 20),
            name="add_up",
        )(parts)

    groups = [[i for i in range(members) if i % 2 == c] for c in range(2)]
    spread = lax.all_to_all(add_up(parts, 1.0, members // 2, BF16), "seq", 0, 0, axis_index_groups=groups, tiled=True)
    total = add_up(spread, 0.125 / (cotangent.shape[1] * members * shards), 1, F32)[0]
    across = lax.ppermute(total, "seq", swap)
    grad_embed, grad_embed_bias, grad_gain, grad_proj, grad_proj_bias = pl.pallas_call(
        unpack_kernel,
        out_shape=(
            jax.ShapeDtypeStruct(embed_weight.shape, F32),
            jax.ShapeDtypeStruct((1, block), F32),
            jax.ShapeDtypeStruct((1, block), F32),
            jax.ShapeDtypeStruct((block, d1), F32),
            jax.ShapeDtypeStruct((1, per), F32),
        ),
        in_specs=[SMEM, VMEM, VMEM],
        out_specs=(VMEM,) * 5,
        scratch_shapes=[pltpu.VMEM((LANES, LANES), F32)],
        compiler_params=pltpu.CompilerParams(vmem_limit_bytes=4 << 20),
        name="unpack",
    )(core, total, across)
    return (pooled[None], grad_embed, grad_embed_bias[0], grad_gain[0], grad_proj, grad_proj_bias[0])


def solution(mesh):
    placed = (
        P("dp", "seq"),
        P(None, None, "dp"),
        P("dp"),
        P("dp"),
        P("dp", None),
        P("dp"),
        P("dp", "seq", None),
    )
    return jax.shard_map(
        local,
        mesh=mesh,
        in_specs=placed,
        out_specs=(
            P("dp", "seq", None),
            P(None, None, "dp"),
            P("dp"),
            P("dp"),
            P("dp", None),
            P("dp"),
        ),
        check_vma=False,
    )
```

```python
import functools

import jax
import jax.numpy as jnp
from jax import lax
from jax.experimental import pallas as pl
from jax.experimental.pallas import tpu as pltpu
from jax.sharding import PartitionSpec as P

F32, BF16 = jnp.float32, jnp.bfloat16
LANES = 128
GELU_A = 0.7978845608028654
GELU_B = 0.044715
GELU_K = (GELU_A * GELU_B) ** (1 / 3)
GELU_C = GELU_A / GELU_K
EPSILON = 1e-06


def dot(a, b, contract, precision=None):
    return lax.dot_general(a, b, ((contract[:1], contract[1:]), ((), ())), precision=precision, preferred_element_type=F32)


def iota(shape, dim):
    return lax.broadcasted_iota(jnp.int32, shape, dim)


def step_kernel(dims, core_ref, inner_ref, bases_ref, outer_ref, own_ref, other_ref, cot_ref,
                pooled_ref, mine_ref, theirs_ref,
                w_ref, code_ref, perm_ref, feat_ref, we_ref, wide_ref, emb_ref, ga_ref, s_ref, ge_ref, gew_ref):
    kw, shards, d0, d1, rows, tile, chunk = dims
    half = w_ref.shape[1] // 2
    pairs, pair_tile = rows // 2, tile // 2
    reach = kw // 2
    taps = kw * 4
    core = core_ref[0]
    per = d1 // shards
    block = d0 // shards

    @pl.when(core == 0)
    def _():
        w_ref[:, :half] = own_ref[...]
        w_ref[:, half:] = other_ref[...]
        code_ref[:, :LANES] = outer_ref[...].astype(F32)
        code_ref[:, LANES + rows:] = inner_ref[...].astype(F32)

    @pl.when(core != 0)
    def _():
        w_ref[:, :half] = other_ref[...]
        w_ref[:, half:] = own_ref[...]
        code_ref[:, :LANES] = inner_ref[...].astype(F32)
        code_ref[:, LANES + rows:] = outer_ref[...].astype(F32)

    code_ref[:, LANES:LANES + rows] = (bases_ref[...] + 1).astype(F32)

    wide = w_ref[:, d1:].astype(F32)
    wide_ref[...] = wide
    we_ref[...] = wide.T.astype(BF16)
    gain = we_ref[pl.ds(64 - 8, 8), :].astype(F32)[5:6, :]
    gain_y = gain * GELU_K

    column = iota((LANES, d1), 1)
    owner = (column * 2341) >> 16
    spread = (iota((LANES, d1), 0) == column - owner * per + 64).astype(F32)
    owned = owner[:shards] == iota((shards, d1), 0)
    pieces = wide_ref[pl.ds(0, shards, stride=block), :]
    bias = jnp.sum(jnp.where(owned, dot(pieces.astype(BF16), spread.astype(BF16), (1, 0)), 0.0), axis=0, keepdims=True)

    source, place = iota((tile, tile), 0), iota((tile, tile), 1)
    perm_ref[...] = (source == jnp.where(place < pair_tile, 2 * place, 2 * (place - pair_tile) + 1)).astype(BF16)
    repeat = ((iota((LANES, 16), 0) >> 2) == iota((LANES, 16), 1)).astype(BF16)
    letter = (iota((LANES, tile), 0) & 3) + 1
    line = iota((LANES, tile), 0)
    for t in range(rows // tile):
        window = code_ref[:, t * tile:t * tile + tile + 2 * LANES]
        start = LANES - reach
        shifted = jnp.concatenate([window[:, start + k:start + k + tile] for k in range(kw)] + [jnp.zeros((1, tile), F32)], axis=0)
        spreaded = dot(repeat, shifted.astype(BF16), (1, 0))
        hot = ((spreaded == letter.astype(F32)) & (line < taps)) | (line == taps)
        ordered = dot(hot.astype(F32).astype(BF16), perm_ref[...], (1, 0))
        feat_ref[:, t * tile:(t + 1) * tile] = ordered.astype(BF16)

    for t in range(rows // tile):
        at = t * tile
        emb_ref[at:at + tile, :] = dot(feat_ref[:, at:at + tile], we_ref[...], (0, 0)).astype(BF16)
        half_at = t * pair_tile
        ga_ref[half_at:half_at + pair_tile, :] = dot(cot_ref[half_at:half_at + pair_tile, :], w_ref[:, :d1], (1, 1))

        def side(start, grad):
            values = emb_ref[pl.ds(start, chunk), :].astype(F32)
            inverse = lax.rsqrt(jnp.sum(values * values, axis=1, keepdims=True) * (1.0 / d0) + EPSILON)
            y = (values * inverse) * gain_y
            square = y * y
            tanh = jnp.tanh(y * (GELU_C + square))
            above, below = 1.0 + tanh, 1.0 - tanh
            activated = y * above
            slope = above + (activated * below) * (GELU_C + 3.0 * square)
            grad_normed = grad * slope
            toward_gain = grad_normed * y
            shared = jnp.sum(toward_gain, axis=1, keepdims=True) * (inverse * inverse * (1.0 / (GELU_K * d0)))
            ge_ref[pl.ds(start, chunk), :] = (inverse * (grad_normed * gain) - values * shared).astype(BF16)
            return activated, toward_gain

        def body(i, total):
            first = pl.multiple_of(at + i * chunk, chunk)
            second = pl.multiple_of(at + pair_tile + i * chunk, chunk)
            pair_at = pl.multiple_of(half_at + i * chunk, chunk)
            grad = ga_ref[pl.ds(pair_at, chunk), :]
            act_even, gain_even = side(first, grad)
            act_odd, gain_odd = side(second, grad)
            s_ref[pl.ds(pair_at, chunk), :] = (act_even + act_odd).astype(BF16)
            both = gain_even + gain_odd
            for r in range(0, chunk, 8):
                total = total + both[r:r + 8]
            return total

        start_total = jnp.zeros((8, d0), F32)
        gain_total = lax.fori_loop(0, pair_tile // chunk, body, start_total, unroll=True)
        pooled_ref[half_at:half_at + pair_tile, :] = (
            (0.25 / GELU_K) * dot(s_ref[half_at:half_at + pair_tile, :], w_ref[:, :d1], (1, 0)) + bias).astype(BF16)
        part = dot(feat_ref[:, at:at + tile], ge_ref[at:at + tile, :], (1, 0))
        is_gain = iota((LANES, d0), 0) == taps + 1
        part = jnp.where(is_gain, jnp.sum(gain_total, axis=0, keepdims=True) / gain_y, part)
        if t == 0:
            gew_ref[...] = part
        else:
            gew_ref[...] += part

    wide_ref[...] = gew_ref[...].T
    sums = 4.0 * jnp.sum(cot_ref[...].astype(F32), axis=0, keepdims=True)
    pieces = dot(jnp.where(owned, sums, 0.0), spread, (1, 1), lax.Precision.HIGHEST)
    wide_ref[pl.ds(0, shards, stride=block), :] = wide_ref[pl.ds(0, shards, stride=block), :] + pieces

    def halves(first_ref, second_ref):
        first_ref[...] = (dot(s_ref[...], cot_ref[:, :half], (0, 0)) * (1.0 / GELU_K)).astype(first_ref.dtype)
        second_ref[:, :d1 - half] = (dot(s_ref[...], cot_ref[:, half:], (0, 0)) * (1.0 / GELU_K)).astype(second_ref.dtype)
        second_ref[:, d1 - half:] = wide_ref[...].astype(second_ref.dtype)

    @pl.when(core == 0)
    def _():
        halves(mine_ref, theirs_ref)

    @pl.when(core != 0)
    def _():
        halves(theirs_ref, mine_ref)


def train_step(core, inner, bases, outer, own, other, cot, kw, shards):
    d0, half = own.shape
    pairs, d1 = cot.shape
    rows = 2 * pairs
    width = 2 * half
    tile, chunk = 512, 32
    dims = (kw, shards, d0, d1, rows, tile, chunk)
    vmem = pl.BlockSpec(memory_space=pltpu.VMEM)
    return pl.pallas_call(
        functools.partial(step_kernel, dims),
        out_shape=(
            jax.ShapeDtypeStruct((pairs, d1), BF16),
            jax.ShapeDtypeStruct((d0, half), F32),
            jax.ShapeDtypeStruct((d0, half), BF16),
        ),
        in_specs=[pl.BlockSpec(memory_space=pltpu.SMEM)] + [vmem] * 6,
        out_specs=(vmem, vmem, vmem),
        scratch_shapes=[
            pltpu.VMEM((d0, width), BF16),
            pltpu.VMEM((1, rows + 2 * LANES), F32),
            pltpu.VMEM((tile, tile), BF16),
            pltpu.VMEM((LANES, rows), BF16),
            pltpu.VMEM((LANES, d0), BF16),
            pltpu.VMEM((d0, LANES), F32),
            pltpu.VMEM((rows, d0), BF16),
            pltpu.VMEM((pairs, d0), F32),
            pltpu.VMEM((pairs, d0), BF16),
            pltpu.VMEM((rows, d0), BF16),
            pltpu.VMEM((LANES, d0), F32),
        ],
        compiler_params=pltpu.CompilerParams(vmem_limit_bytes=28 << 20),
        name="train_step",
    )(core, inner, bases, outer, own, other, cot)


def pack_kernel(core_ref, bases_hbm, embed_hbm, embed_bias_hbm, gain_hbm, proj_hbm, proj_bias_hbm,
                out_ref, inner_ref, outer_ref,
                bases_ref, embed_ref, embed_bias_ref, gain_ref, proj_ref, proj_bias_ref, rows_ref, block_ref, sems):
    kw, block, d1 = embed_ref.shape[0], proj_ref.shape[0], proj_ref.shape[1]
    copies, _, half = out_ref.shape
    taps, per = kw * 4, proj_bias_ref.shape[1]
    fetched = [
        pltpu.make_async_copy(source, target, sems.at[n])
        for n, (source, target) in enumerate((
            (bases_hbm, bases_ref), (embed_hbm, embed_ref), (embed_bias_hbm, embed_bias_ref),
            (gain_hbm, gain_ref), (proj_hbm, proj_ref), (proj_bias_hbm, proj_bias_ref)))
    ]
    for copy in fetched:
        copy.start()
    rows_ref[...] = jnp.zeros_like(rows_ref)
    for copy in fetched:
        copy.wait()
    first = bases_ref[:, :LANES] + 1
    last = bases_ref[:, bases_ref.shape[1] - LANES:] + 1
    even = core_ref[0] == 0
    inner_ref[...] = jnp.where(even, last, first)
    outer_ref[...] = jnp.where(even, first, last)
    for k in range(kw):
        rows_ref[4 * k:4 * k + 4, :block] = embed_ref[k].astype(F32)
    rows_ref[taps:taps + 1, :block] = embed_bias_ref[...].astype(F32)
    rows_ref[taps + 1:taps + 2, :block] = gain_ref[...].astype(F32)
    block_ref[...] = rows_ref[...].T[:block]
    block_ref[:1, 64:64 + per] = proj_bias_ref[...].astype(F32)
    edge = d1 - half

    @pl.when(even)
    def _():
        for i in range(copies):
            out_ref[i] = proj_ref[:, :half]

    @pl.when(jnp.logical_not(even))
    def _():
        for i in range(copies):
            out_ref[i, :, :edge] = proj_ref[:, half:]
            out_ref[i, :, edge:] = block_ref[...].astype(BF16)


def sum_kernel(scale, in_ref, out_ref):
    total = in_ref[0].astype(F32)
    for i in range(1, in_ref.shape[0]):
        total = total + in_ref[i].astype(F32)
    if scale != 1.0:
        total = total * scale
    total = total.astype(out_ref.dtype)
    for i in range(out_ref.shape[0]):
        out_ref[i] = total


def unpack_kernel(core_ref, total_ref, across_ref, embed_ref, embed_bias_ref, gain_ref, proj_ref, proj_bias_ref, rows_ref):
    kw, block, d1 = embed_ref.shape[0], proj_ref.shape[0], proj_ref.shape[1]
    half = total_ref.shape[1]
    taps, per, edge = kw * 4, proj_bias_ref.shape[1], d1 - half

    def place(left_ref, right_ref):
        proj_ref[:, :half] = left_ref[...]
        proj_ref[:, half:] = right_ref[:, :edge]
        rows_ref[:block, :] = right_ref[:, edge:]

    @pl.when(core_ref[0] == 0)
    def _():
        place(total_ref, across_ref)

    @pl.when(core_ref[0] != 0)
    def _():
        place(across_ref, total_ref)

    proj_bias_ref[...] = rows_ref[:1, 64:64 + per]
    rows_ref[block:, :] = jnp.zeros((LANES - block, LANES), F32)
    rows_ref[...] = rows_ref[...].T
    for k in range(kw):
        embed_ref[k] = rows_ref[4 * k:4 * k + 4, :block]
    embed_bias_ref[...] = rows_ref[taps:taps + 1, :block]
    gain_ref[...] = rows_ref[taps + 1:taps + 2, :block]


VMEM = pl.BlockSpec(memory_space=pltpu.VMEM)
SMEM = pl.BlockSpec(memory_space=pltpu.SMEM)


def local(bases, embed_weight, embed_bias, norm_gain, proj_weight, proj_bias, cotangent):
    kw = embed_weight.shape[0]
    shards, members = lax.axis_size("dp"), lax.axis_size("seq")
    block, d1 = proj_weight.shape
    per = proj_bias.shape[0]
    half = (d1 + LANES) // 2
    core = (lax.axis_index("seq") & 1).astype(jnp.int32).reshape(1)
    swap = [(i, i ^ 1) for i in range(members)]

    facing = [(i, i + 1 if i % 2 else i - 1) for i in range(1, members - 1)]

    hbm = pl.BlockSpec(memory_space=pltpu.HBM)
    gathered = (bases, embed_weight, embed_bias[None], norm_gain[None], proj_weight, proj_bias[None])
    piece, inner, outer = pl.pallas_call(
        pack_kernel,
        out_shape=(
            jax.ShapeDtypeStruct((shards, block, half), BF16),
            jax.ShapeDtypeStruct((1, LANES), jnp.int32),
            jax.ShapeDtypeStruct((1, LANES), jnp.int32),
        ),
        in_specs=[SMEM] + [hbm] * 6,
        out_specs=(VMEM,) * 3,
        scratch_shapes=[pltpu.VMEM(x.shape, x.dtype) for x in gathered] + [
            pltpu.VMEM((LANES, LANES), F32), pltpu.VMEM((block, LANES), F32), pltpu.SemaphoreType.DMA((6,))],
        compiler_params=pltpu.CompilerParams(vmem_limit_bytes=60 << 20),
        name="pack",
    )(core, *gathered)
    inner = lax.ppermute(inner, "seq", swap)
    outer = lax.ppermute(outer, "seq", facing)
    own = lax.all_to_all(piece, "dp", 0, 0, tiled=True).reshape(shards * block, half)
    own, inner, outer = lax.optimization_barrier((own, inner, outer))
    other = lax.ppermute(own, "seq", swap)

    pooled, mine, theirs = train_step(core, inner, bases, outer, own, other, cotangent[0], kw, shards)

    came = lax.ppermute(theirs, "seq", swap)
    summed = (mine + came.astype(F32)).astype(BF16).reshape(shards, block, half)
    parts = lax.all_to_all(summed, "dp", 0, 0, tiled=True)

    def add_up(parts, scale, copies, kind):
        return pl.pallas_call(
            functools.partial(sum_kernel, scale),
            out_shape=jax.ShapeDtypeStruct((copies, block, half), kind),
            in_specs=[VMEM],
            out_specs=VMEM,
            compiler_params=pltpu.CompilerParams(vmem_limit_bytes=4 << 20),
            name="add_up",
        )(parts)

    groups = [[i for i in range(members) if i % 2 == c] for c in range(2)]
    spread = lax.all_to_all(add_up(parts, 1.0, members // 2, BF16), "seq", 0, 0, axis_index_groups=groups, tiled=True)
    total = add_up(spread, 0.125 / (cotangent.shape[1] * members * shards), 1, F32)[0]
    across = lax.ppermute(total, "seq", swap)
    grad_embed, grad_embed_bias, grad_gain, grad_proj, grad_proj_bias = pl.pallas_call(
        unpack_kernel,
        out_shape=(
            jax.ShapeDtypeStruct(embed_weight.shape, F32),
            jax.ShapeDtypeStruct((1, block), F32),
            jax.ShapeDtypeStruct((1, block), F32),
            jax.ShapeDtypeStruct((block, d1), F32),
            jax.ShapeDtypeStruct((1, per), F32),
        ),
        in_specs=[SMEM, VMEM, VMEM],
        out_specs=(VMEM,) * 5,
        scratch_shapes=[pltpu.VMEM((LANES, LANES), F32)],
        compiler_params=pltpu.CompilerParams(vmem_limit_bytes=4 << 20),
        name="unpack",
    )(core, total, across)
    return (pooled[None], grad_embed, grad_embed_bias[0], grad_gain[0], grad_proj, grad_proj_bias[0])


def solution(mesh):
    placed = (
        P("dp", "seq"),
        P(None, None, "dp"),
        P("dp"),
        P("dp"),
        P("dp", None),
        P("dp"),
        P("dp", "seq", None),
    )
    return jax.shard_map(
        local,
        mesh=mesh,
        in_specs=placed,
        out_specs=(
            P("dp", "seq", None),
            P(None, None, "dp"),
            P("dp"),
            P("dp"),
            P("dp", None),
            P("dp"),
        ),
        check_vma=False,
    )
```

```python
import functools

import jax
import jax.numpy as jnp
from jax import lax
from jax.experimental import pallas as pl
from jax.experimental.pallas import tpu as pltpu
from jax.sharding import PartitionSpec as P

F32, BF16 = jnp.float32, jnp.bfloat16
LANES = 128
GELU_A = 0.7978845608028654
GELU_B = 0.044715
GELU_K = (GELU_A * GELU_B) ** (1 / 3)
GELU_C = GELU_A / GELU_K
EPSILON = 1e-06


def dot(a, b, contract, precision=None):
    return lax.dot_general(a, b, ((contract[:1], contract[1:]), ((), ())), precision=precision, preferred_element_type=F32)


def iota(shape, dim):
    return lax.broadcasted_iota(jnp.int32, shape, dim)


def by_owner(shards, d1):
    per = d1 // shards
    column = iota((LANES, d1), 1)
    owner = (column * 2341) >> 16
    spread = (iota((LANES, d1), 0) == column - owner * per + 64).astype(F32)
    return owner[:shards] == iota((shards, d1), 0), spread


def feature_kernel(kw, tile, core_ref, inner_ref, bases_ref, outer_ref, cot_ref, feat_ref, sums_ref, code_ref, perm_ref):
    rows = bases_ref.shape[1]
    pair_tile, reach, taps = tile // 2, kw // 2, kw * 4

    @pl.when(core_ref[0] == 0)
    def _():
        code_ref[:, :LANES] = outer_ref[...].astype(F32)
        code_ref[:, LANES + rows:] = inner_ref[...].astype(F32)

    @pl.when(core_ref[0] != 0)
    def _():
        code_ref[:, :LANES] = inner_ref[...].astype(F32)
        code_ref[:, LANES + rows:] = outer_ref[...].astype(F32)

    code_ref[:, LANES:LANES + rows] = (bases_ref[...] + 1).astype(F32)
    source, place = iota((tile, tile), 0), iota((tile, tile), 1)
    perm_ref[...] = (source == jnp.where(place < pair_tile, 2 * place, 2 * (place - pair_tile) + 1)).astype(BF16)
    repeat = ((iota((LANES, 16), 0) >> 2) == iota((LANES, 16), 1)).astype(BF16)
    letter = (iota((LANES, tile), 0) & 3) + 1
    line = iota((LANES, tile), 0)
    for t in range(rows // tile):
        window = code_ref[:, t * tile:t * tile + tile + 2 * LANES]
        start = LANES - reach
        shifted = jnp.concatenate([window[:, start + k:start + k + tile] for k in range(kw)] + [jnp.zeros((1, tile), F32)], axis=0)
        spreaded = dot(repeat, shifted.astype(BF16), (1, 0))
        hot = ((spreaded == letter.astype(F32)) & (line < taps)) | (line == taps)
        ordered = dot(hot.astype(F32).astype(BF16), perm_ref[...], (1, 0))
        feat_ref[:, t * tile:(t + 1) * tile] = ordered.astype(BF16)

    shards = sums_ref.shape[0]
    owned, spread = by_owner(shards, cot_ref.shape[1])
    sums = 4.0 * jnp.sum(cot_ref[...].astype(F32), axis=0, keepdims=True)
    sums_ref[...] = dot(jnp.where(owned, sums, 0.0), spread, (1, 1), lax.Precision.HIGHEST)


def step_kernel(dims, core_ref, feat_ref, sums_ref, own_ref, other_ref, cot_ref,
                theirs_ref, s_ref, wide_ref, bias_ref,
                w_ref, we_ref, emb_ref, ga_ref, ge_ref, gew_ref):
    kw, shards, d0, d1, rows, tile, chunk = dims
    half = w_ref.shape[1] // 2
    pair_tile = tile // 2
    taps = kw * 4
    core = core_ref[0]
    block = d0 // shards

    @pl.when(core == 0)
    def _():
        w_ref[:, :half] = own_ref[...]
        w_ref[:, half:] = other_ref[...]

    @pl.when(core != 0)
    def _():
        w_ref[:, :half] = other_ref[...]
        w_ref[:, half:] = own_ref[...]

    wide = w_ref[:, d1:].astype(F32)
    wide_ref[...] = wide
    we_ref[...] = wide.T.astype(BF16)
    gain = we_ref[pl.ds(64 - 8, 8), :].astype(F32)[5:6, :]
    gain_y = gain * GELU_K

    owned, spread = by_owner(shards, d1)
    pieces = wide_ref[pl.ds(0, shards, stride=block), :]
    bias_ref[...] = jnp.sum(jnp.where(owned, dot(pieces.astype(BF16), spread.astype(BF16), (1, 0)), 0.0), axis=0, keepdims=True)

    for t in range(rows // tile):
        at = t * tile
        emb_ref[at:at + tile, :] = dot(feat_ref[:, at:at + tile], we_ref[...], (0, 0)).astype(BF16)
        half_at = t * pair_tile
        ga_ref[half_at:half_at + pair_tile, :] = dot(cot_ref[half_at:half_at + pair_tile, :], w_ref[:, :d1], (1, 1))

        def side(start, grad):
            values = emb_ref[pl.ds(start, chunk), :].astype(F32)
            inverse = lax.rsqrt(jnp.sum(values * values, axis=1, keepdims=True) * (1.0 / d0) + EPSILON)
            y = (values * inverse) * gain_y
            square = y * y
            tanh = jnp.tanh(y * (GELU_C + square))
            above, below = 1.0 + tanh, 1.0 - tanh
            activated = y * above
            slope = above + (activated * below) * (GELU_C + 3.0 * square)
            grad_normed = grad * slope
            toward_gain = grad_normed * y
            shared = jnp.sum(toward_gain, axis=1, keepdims=True) * (inverse * inverse * (1.0 / (GELU_K * d0)))
            ge_ref[pl.ds(start, chunk), :] = (inverse * (grad_normed * gain) - values * shared).astype(BF16)
            return activated, toward_gain

        def body(i, total):
            first = pl.multiple_of(at + i * chunk, chunk)
            second = pl.multiple_of(at + pair_tile + i * chunk, chunk)
            pair_at = pl.multiple_of(half_at + i * chunk, chunk)
            grad = ga_ref[pl.ds(pair_at, chunk), :]
            act_even, gain_even = side(first, grad)
            act_odd, gain_odd = side(second, grad)
            s_ref[pl.ds(pair_at, chunk), :] = (act_even + act_odd).astype(BF16)
            both = gain_even + gain_odd
            for r in range(0, chunk, 8):
                total = total + both[r:r + 8]
            return total

        start_total = jnp.zeros((8, d0), F32)
        gain_total = lax.fori_loop(0, pair_tile // chunk, body, start_total, unroll=True)
        part = dot(feat_ref[:, at:at + tile], ge_ref[at:at + tile, :], (1, 0))
        is_gain = iota((LANES, d0), 0) == taps + 1
        part = jnp.where(is_gain, jnp.sum(gain_total, axis=0, keepdims=True) / gain_y, part)
        if t == 0:
            gew_ref[...] = part
        else:
            gew_ref[...] += part

    wide_ref[...] = gew_ref[...].T
    wide_ref[pl.ds(0, shards, stride=block), :] = wide_ref[pl.ds(0, shards, stride=block), :] + sums_ref[...]

    @pl.when(core == 0)
    def _():
        right_half(s_ref, cot_ref, wide_ref, theirs_ref)

    @pl.when(core != 0)
    def _():
        left_half(s_ref, cot_ref, theirs_ref)


def left_half(s_ref, cot_ref, out_ref):
    half = out_ref.shape[1]
    out_ref[...] = (dot(s_ref[...], cot_ref[:, :half], (0, 0)) * (1.0 / GELU_K)).astype(out_ref.dtype)


def right_half(s_ref, cot_ref, wide_ref, out_ref):
    half = out_ref.shape[1]
    edge = cot_ref.shape[1] - half
    out_ref[:, :edge] = (dot(s_ref[...], cot_ref[:, half:], (0, 0)) * (1.0 / GELU_K)).astype(out_ref.dtype)
    out_ref[:, edge:] = wide_ref[...].astype(out_ref.dtype)


def keep_kernel(core_ref, s_ref, cot_ref, wide_ref, mine_ref):
    @pl.when(core_ref[0] == 0)
    def _():
        left_half(s_ref, cot_ref, mine_ref)

    @pl.when(core_ref[0] != 0)
    def _():
        right_half(s_ref, cot_ref, wide_ref, mine_ref)


def pool_kernel(core_ref, s_ref, own_ref, other_ref, bias_ref, pooled_ref):
    half = own_ref.shape[1]
    edge = pooled_ref.shape[1] - half

    def project(left_ref, right_ref):
        pooled_ref[:, :half] = ((0.25 / GELU_K) * dot(s_ref[...], left_ref[...], (1, 0)) + bias_ref[:, :half]).astype(BF16)
        pooled_ref[:, half:] = ((0.25 / GELU_K) * dot(s_ref[...], right_ref[:, :edge], (1, 0)) + bias_ref[:, half:]).astype(BF16)

    @pl.when(core_ref[0] == 0)
    def _():
        project(own_ref, other_ref)

    @pl.when(core_ref[0] != 0)
    def _():
        project(other_ref, own_ref)


VMEM = pl.BlockSpec(memory_space=pltpu.VMEM)
SMEM = pl.BlockSpec(memory_space=pltpu.SMEM)
TILE, CHUNK = 512, 32


def make_features(core, inner, bases, outer, cot, kw, shards):
    rows = bases.shape[1]
    return pl.pallas_call(
        functools.partial(feature_kernel, kw, TILE),
        out_shape=(jax.ShapeDtypeStruct((LANES, rows), BF16), jax.ShapeDtypeStruct((shards, LANES), F32)),
        in_specs=[SMEM] + [VMEM] * 4,
        out_specs=(VMEM, VMEM),
        scratch_shapes=[pltpu.VMEM((1, rows + 2 * LANES), F32), pltpu.VMEM((TILE, TILE), BF16)],
        compiler_params=pltpu.CompilerParams(vmem_limit_bytes=16 << 20),
        cost_estimate=pl.CostEstimate(flops=2 * LANES * TILE * rows, bytes_accessed=2 << 20, transcendentals=0),
        name="features",
    )(core, inner, bases, outer, cot)


def backward(core, feat, sums, own, other, cot, kw, shards):
    d0, half = own.shape
    pairs, d1 = cot.shape
    rows = 2 * pairs
    dims = (kw, shards, d0, d1, rows, TILE, CHUNK)
    return pl.pallas_call(
        functools.partial(step_kernel, dims),
        out_shape=(
            jax.ShapeDtypeStruct((d0, half), BF16),
            jax.ShapeDtypeStruct((pairs, d0), BF16),
            jax.ShapeDtypeStruct((d0, LANES), F32),
            jax.ShapeDtypeStruct((1, d1), F32),
        ),
        in_specs=[SMEM] + [VMEM] * 5,
        out_specs=(VMEM,) * 4,
        scratch_shapes=[
            pltpu.VMEM((d0, 2 * half), BF16),
            pltpu.VMEM((LANES, d0), BF16),
            pltpu.VMEM((rows, d0), BF16),
            pltpu.VMEM((pairs, d0), F32),
            pltpu.VMEM((rows, d0), BF16),
            pltpu.VMEM((LANES, d0), F32),
        ],
        compiler_params=pltpu.CompilerParams(vmem_limit_bytes=28 << 20),
        cost_estimate=pl.CostEstimate(flops=6 * pairs * d0 * d1, bytes_accessed=6 << 20, transcendentals=rows * d0),
        name="backward",
    )(core, feat, sums, own, other, cot)


def keep_half(core, s, cot, wide, half):
    pairs, d0 = s.shape
    return pl.pallas_call(
        keep_kernel,
        out_shape=jax.ShapeDtypeStruct((d0, half), F32),
        in_specs=[SMEM] + [VMEM] * 3,
        out_specs=VMEM,
        compiler_params=pltpu.CompilerParams(vmem_limit_bytes=16 << 20),
        cost_estimate=pl.CostEstimate(flops=2 * pairs * d0 * half, bytes_accessed=4 << 20, transcendentals=0),
        name="keep_half",
    )(core, s, cot, wide)


def pool(core, s, own, other, bias):
    pairs, d0 = s.shape
    d1 = bias.shape[1]
    return pl.pallas_call(
        pool_kernel,
        out_shape=jax.ShapeDtypeStruct((pairs, d1), BF16),
        in_specs=[SMEM] + [VMEM] * 4,
        out_specs=VMEM,
        compiler_params=pltpu.CompilerParams(vmem_limit_bytes=16 << 20),
        cost_estimate=pl.CostEstimate(flops=2 * pairs * d0 * d1, bytes_accessed=4 << 20, transcendentals=0),
        name="pool",
    )(core, s, own, other, bias)


def pack_kernel(core_ref, bases_hbm, embed_hbm, embed_bias_hbm, gain_hbm, proj_hbm, proj_bias_hbm,
                out_ref, inner_ref, outer_ref,
                bases_ref, embed_ref, embed_bias_ref, gain_ref, proj_ref, proj_bias_ref, rows_ref, block_ref, sems):
    kw, block, d1 = embed_ref.shape[0], proj_ref.shape[0], proj_ref.shape[1]
    copies, _, half = out_ref.shape
    taps, per = kw * 4, proj_bias_ref.shape[1]
    fetched = [
        pltpu.make_async_copy(source, target, sems.at[n])
        for n, (source, target) in enumerate((
            (bases_hbm, bases_ref), (embed_hbm, embed_ref), (embed_bias_hbm, embed_bias_ref),
            (gain_hbm, gain_ref), (proj_hbm, proj_ref), (proj_bias_hbm, proj_bias_ref)))
    ]
    for copy in fetched:
        copy.start()
    rows_ref[...] = jnp.zeros_like(rows_ref)
    for copy in fetched:
        copy.wait()
    first = bases_ref[:, :LANES] + 1
    last = bases_ref[:, bases_ref.shape[1] - LANES:] + 1
    even = core_ref[0] == 0
    inner_ref[...] = jnp.where(even, last, first)
    outer_ref[...] = jnp.where(even, first, last)
    for k in range(kw):
        rows_ref[4 * k:4 * k + 4, :block] = embed_ref[k].astype(F32)
    rows_ref[taps:taps + 1, :block] = embed_bias_ref[...].astype(F32)
    rows_ref[taps + 1:taps + 2, :block] = gain_ref[...].astype(F32)
    block_ref[...] = rows_ref[...].T[:block]
    block_ref[:1, 64:64 + per] = proj_bias_ref[...].astype(F32)
    edge = d1 - half

    @pl.when(even)
    def _():
        for i in range(copies):
            out_ref[i] = proj_ref[:, :half]

    @pl.when(jnp.logical_not(even))
    def _():
        for i in range(copies):
            out_ref[i, :, :edge] = proj_ref[:, half:]
            out_ref[i, :, edge:] = block_ref[...].astype(BF16)


def sum_kernel(scale, in_ref, out_ref):
    total = in_ref[0].astype(F32)
    for i in range(1, in_ref.shape[0]):
        total = total + in_ref[i].astype(F32)
    if scale != 1.0:
        total = total * scale
    total = total.astype(out_ref.dtype)
    for i in range(out_ref.shape[0]):
        out_ref[i] = total


def unpack_kernel(core_ref, total_ref, across_ref, embed_ref, embed_bias_ref, gain_ref, proj_ref, proj_bias_ref, rows_ref):
    kw, block, d1 = embed_ref.shape[0], proj_ref.shape[0], proj_ref.shape[1]
    half = total_ref.shape[1]
    taps, per, edge = kw * 4, proj_bias_ref.shape[1], d1 - half

    def place(left_ref, right_ref):
        proj_ref[:, :half] = left_ref[...]
        proj_ref[:, half:] = right_ref[:, :edge]
        rows_ref[:block, :] = right_ref[:, edge:]

    @pl.when(core_ref[0] == 0)
    def _():
        place(total_ref, across_ref)

    @pl.when(core_ref[0] != 0)
    def _():
        place(across_ref, total_ref)

    proj_bias_ref[...] = rows_ref[:1, 64:64 + per]
    rows_ref[block:, :] = jnp.zeros((LANES - block, LANES), F32)
    rows_ref[...] = rows_ref[...].T
    for k in range(kw):
        embed_ref[k] = rows_ref[4 * k:4 * k + 4, :block]
    embed_bias_ref[...] = rows_ref[taps:taps + 1, :block]
    gain_ref[...] = rows_ref[taps + 1:taps + 2, :block]


def local(bases, embed_weight, embed_bias, norm_gain, proj_weight, proj_bias, cotangent):
    kw = embed_weight.shape[0]
    shards, members = lax.axis_size("dp"), lax.axis_size("seq")
    block, d1 = proj_weight.shape
    per = proj_bias.shape[0]
    half = (d1 + LANES) // 2
    core = (lax.axis_index("seq") & 1).astype(jnp.int32).reshape(1)
    swap = [(i, i ^ 1) for i in range(members)]

    facing = [(i, i + 1 if i % 2 else i - 1) for i in range(1, members - 1)]

    hbm = pl.BlockSpec(memory_space=pltpu.HBM)
    gathered = (bases, embed_weight, embed_bias[None], norm_gain[None], proj_weight, proj_bias[None])
    piece, inner, outer = pl.pallas_call(
        pack_kernel,
        out_shape=(
            jax.ShapeDtypeStruct((shards, block, half), BF16),
            jax.ShapeDtypeStruct((1, LANES), jnp.int32),
            jax.ShapeDtypeStruct((1, LANES), jnp.int32),
        ),
        in_specs=[SMEM] + [hbm] * 6,
        out_specs=(VMEM,) * 3,
        scratch_shapes=[pltpu.VMEM(x.shape, x.dtype) for x in gathered] + [
            pltpu.VMEM((LANES, LANES), F32), pltpu.VMEM((block, LANES), F32), pltpu.SemaphoreType.DMA((6,))],
        compiler_params=pltpu.CompilerParams(vmem_limit_bytes=60 << 20),
        name="pack",
    )(core, *gathered)
    inner = lax.ppermute(inner, "seq", swap)
    outer = lax.ppermute(outer, "seq", facing)
    own = lax.all_to_all(piece, "dp", 0, 0, tiled=True).reshape(shards * block, half)
    feat, sums = make_features(core, inner, bases, outer, cotangent[0], kw, shards)
    own, feat, sums = lax.optimization_barrier((own, feat, sums))
    other = lax.ppermute(own, "seq", swap)

    cot = cotangent[0]
    theirs, s, wide, bias = backward(core, feat, sums, own, other, cot, kw, shards)
    came = lax.ppermute(theirs, "seq", swap)
    mine = keep_half(core, s, cot, wide, half)
    pooled = pool(core, s, own, other, bias)
    summed = (mine + came.astype(F32)).astype(BF16).reshape(shards, block, half)
    parts = lax.all_to_all(summed, "dp", 0, 0, tiled=True)

    def add_up(parts, scale, copies, kind):
        return pl.pallas_call(
            functools.partial(sum_kernel, scale),
            out_shape=jax.ShapeDtypeStruct((copies, block, half), kind),
            in_specs=[VMEM],
            out_specs=VMEM,
            compiler_params=pltpu.CompilerParams(vmem_limit_bytes=4 << 20),
            name="add_up",
        )(parts)

    groups = [[i for i in range(members) if i % 2 == c] for c in range(2)]
    spread = lax.all_to_all(add_up(parts, 1.0, members // 2, BF16), "seq", 0, 0, axis_index_groups=groups, tiled=True)
    total = add_up(spread, 0.125 / (cotangent.shape[1] * members * shards), 1, F32)[0]
    across = lax.ppermute(total, "seq", swap)
    grad_embed, grad_embed_bias, grad_gain, grad_proj, grad_proj_bias = pl.pallas_call(
        unpack_kernel,
        out_shape=(
            jax.ShapeDtypeStruct(embed_weight.shape, F32),
            jax.ShapeDtypeStruct((1, block), F32),
            jax.ShapeDtypeStruct((1, block), F32),
            jax.ShapeDtypeStruct((block, d1), F32),
            jax.ShapeDtypeStruct((1, per), F32),
        ),
        in_specs=[SMEM, VMEM, VMEM],
        out_specs=(VMEM,) * 5,
        scratch_shapes=[pltpu.VMEM((LANES, LANES), F32)],
        compiler_params=pltpu.CompilerParams(vmem_limit_bytes=4 << 20),
        name="unpack",
    )(core, total, across)
    return (pooled[None], grad_embed, grad_embed_bias[0], grad_gain[0], grad_proj, grad_proj_bias[0])


def solution(mesh):
    placed = (
        P("dp", "seq"),
        P(None, None, "dp"),
        P("dp"),
        P("dp"),
        P("dp", None),
        P("dp"),
        P("dp", "seq", None),
    )
    return jax.shard_map(
        local,
        mesh=mesh,
        in_specs=placed,
        out_specs=(
            P("dp", "seq", None),
            P(None, None, "dp"),
            P("dp"),
            P("dp"),
            P("dp", None),
            P("dp"),
        ),
        check_vma=False,
    )
```

```python
import functools

import jax
import jax.numpy as jnp
from jax import lax
from jax.experimental import pallas as pl
from jax.experimental.pallas import tpu as pltpu
from jax.sharding import PartitionSpec as P

F32, BF16 = jnp.float32, jnp.bfloat16
LANES = 128
GELU_A = 0.7978845608028654
GELU_B = 0.044715
GELU_K = (GELU_A * GELU_B) ** (1 / 3)
GELU_C = GELU_A / GELU_K
EPSILON = 1e-06


def dot(a, b, contract, precision=None):
    return lax.dot_general(a, b, ((contract[:1], contract[1:]), ((), ())), precision=precision, preferred_element_type=F32)


def iota(shape, dim):
    return lax.broadcasted_iota(jnp.int32, shape, dim)


def by_owner(shards, d1):
    per = d1 // shards
    column = iota((LANES, d1), 1)
    owner = (column * 2341) >> 16
    spread = (iota((LANES, d1), 0) == column - owner * per + 64).astype(F32)
    return owner[:shards] == iota((shards, d1), 0), spread


def feature_kernel(kw, tile, core_ref, inner_ref, bases_ref, outer_ref, cot_ref, feat_ref, sums_ref, code_ref, perm_ref):
    rows = bases_ref.shape[1]
    pair_tile, reach, taps = tile // 2, kw // 2, kw * 4

    @pl.when(core_ref[0] == 0)
    def _():
        code_ref[:, :LANES] = outer_ref[...].astype(F32)
        code_ref[:, LANES + rows:] = inner_ref[...].astype(F32)

    @pl.when(core_ref[0] != 0)
    def _():
        code_ref[:, :LANES] = inner_ref[...].astype(F32)
        code_ref[:, LANES + rows:] = outer_ref[...].astype(F32)

    code_ref[:, LANES:LANES + rows] = (bases_ref[...] + 1).astype(F32)
    source, place = iota((tile, tile), 0), iota((tile, tile), 1)
    perm_ref[...] = (source == jnp.where(place < pair_tile, 2 * place, 2 * (place - pair_tile) + 1)).astype(BF16)
    repeat = ((iota((LANES, 16), 0) >> 2) == iota((LANES, 16), 1)).astype(BF16)
    letter = (iota((LANES, tile), 0) & 3) + 1
    line = iota((LANES, tile), 0)
    for t in range(rows // tile):
        window = code_ref[:, t * tile:t * tile + tile + 2 * LANES]
        start = LANES - reach
        shifted = jnp.concatenate([window[:, start + k:start + k + tile] for k in range(kw)] + [jnp.zeros((1, tile), F32)], axis=0)
        spreaded = dot(repeat, shifted.astype(BF16), (1, 0))
        hot = ((spreaded == letter.astype(F32)) & (line < taps)) | (line == taps)
        ordered = dot(hot.astype(F32).astype(BF16), perm_ref[...], (1, 0))
        feat_ref[:, t * tile:(t + 1) * tile] = ordered.astype(BF16)

    shards = sums_ref.shape[0]
    owned, spread = by_owner(shards, cot_ref.shape[1])
    sums = 4.0 * jnp.sum(cot_ref[...].astype(F32), axis=0, keepdims=True)
    sums_ref[...] = dot(jnp.where(owned, sums, 0.0), spread, (1, 1), lax.Precision.HIGHEST)


def step_kernel(dims, core_ref, feat_ref, sums_ref, own_ref, other_ref, cot_ref,
                theirs_ref, s_ref, wide_ref, bias_ref,
                w_ref, we_ref, emb_ref, ga_ref, ge_ref, gew_ref):
    kw, shards, d0, d1, rows, tile, chunk = dims
    half = w_ref.shape[1] // 2
    pair_tile = tile // 2
    taps = kw * 4
    core = core_ref[0]
    block = d0 // shards

    @pl.when(core == 0)
    def _():
        w_ref[:, :half] = own_ref[...]
        w_ref[:, half:] = other_ref[...]

    @pl.when(core != 0)
    def _():
        w_ref[:, :half] = other_ref[...]
        w_ref[:, half:] = own_ref[...]

    wide = w_ref[:, d1:].astype(F32)
    wide_ref[...] = wide
    we_ref[...] = wide.T.astype(BF16)
    gain = we_ref[pl.ds(64 - 8, 8), :].astype(F32)[5:6, :]
    gain_y = gain * GELU_K

    owned, spread = by_owner(shards, d1)
    pieces = wide_ref[pl.ds(0, shards, stride=block), :]
    bias_ref[...] = jnp.sum(jnp.where(owned, dot(pieces.astype(BF16), spread.astype(BF16), (1, 0)), 0.0), axis=0, keepdims=True)

    for t in range(rows // tile):
        at = t * tile
        emb_ref[at:at + tile, :] = dot(feat_ref[:, at:at + tile], we_ref[...], (0, 0)).astype(BF16)
        half_at = t * pair_tile
        ga_ref[half_at:half_at + pair_tile, :] = dot(cot_ref[half_at:half_at + pair_tile, :], w_ref[:, :d1], (1, 1))

        def side(start, grad):
            values = emb_ref[pl.ds(start, chunk), :].astype(F32)
            inverse = lax.rsqrt(jnp.sum(values * values, axis=1, keepdims=True) * (1.0 / d0) + EPSILON)
            y = (values * inverse) * gain_y
            square = y * y
            tanh = jnp.tanh(y * (GELU_C + square))
            above, below = 1.0 + tanh, 1.0 - tanh
            activated = y * above
            slope = above + (activated * below) * (GELU_C + 3.0 * square)
            grad_normed = grad * slope
            toward_gain = grad_normed * y
            shared = jnp.sum(toward_gain, axis=1, keepdims=True) * (inverse * inverse * (1.0 / (GELU_K * d0)))
            ge_ref[pl.ds(start, chunk), :] = (inverse * (grad_normed * gain) - values * shared).astype(BF16)
            return activated, toward_gain

        def body(i, total):
            first = pl.multiple_of(at + i * chunk, chunk)
            second = pl.multiple_of(at + pair_tile + i * chunk, chunk)
            pair_at = pl.multiple_of(half_at + i * chunk, chunk)
            grad = ga_ref[pl.ds(pair_at, chunk), :]
            act_even, gain_even = side(first, grad)
            act_odd, gain_odd = side(second, grad)
            s_ref[pl.ds(pair_at, chunk), :] = (act_even + act_odd).astype(BF16)
            both = gain_even + gain_odd
            for r in range(0, chunk, 8):
                total = total + both[r:r + 8]
            return total

        start_total = jnp.zeros((8, d0), F32)
        gain_total = lax.fori_loop(0, pair_tile // chunk, body, start_total, unroll=True)
        part = dot(feat_ref[:, at:at + tile], ge_ref[at:at + tile, :], (1, 0))
        is_gain = iota((LANES, d0), 0) == taps + 1
        part = jnp.where(is_gain, jnp.sum(gain_total, axis=0, keepdims=True) / gain_y, part)
        if t == 0:
            gew_ref[...] = part
        else:
            gew_ref[...] += part

    wide_ref[...] = gew_ref[...].T
    wide_ref[pl.ds(0, shards, stride=block), :] = wide_ref[pl.ds(0, shards, stride=block), :] + sums_ref[...]

    @pl.when(core == 0)
    def _():
        right_half(s_ref, cot_ref, wide_ref, theirs_ref)

    @pl.when(core != 0)
    def _():
        left_half(s_ref, cot_ref, theirs_ref)


def left_half(s_ref, cot_ref, out_ref):
    half = out_ref.shape[1]
    out_ref[...] = (dot(s_ref[...], cot_ref[:, :half], (0, 0)) * (1.0 / GELU_K)).astype(out_ref.dtype)


def right_half(s_ref, cot_ref, wide_ref, out_ref):
    half = out_ref.shape[1]
    edge = cot_ref.shape[1] - half
    out_ref[:, :edge] = (dot(s_ref[...], cot_ref[:, half:], (0, 0)) * (1.0 / GELU_K)).astype(out_ref.dtype)
    out_ref[:, edge:] = wide_ref[...].astype(out_ref.dtype)


def keep_kernel(core_ref, s_ref, cot_ref, wide_ref, mine_ref):
    @pl.when(core_ref[0] == 0)
    def _():
        left_half(s_ref, cot_ref, mine_ref)

    @pl.when(core_ref[0] != 0)
    def _():
        right_half(s_ref, cot_ref, wide_ref, mine_ref)


def pool_kernel(core_ref, s_ref, own_ref, other_ref, bias_ref, pooled_ref):
    half = own_ref.shape[1]
    edge = pooled_ref.shape[1] - half

    def project(left_ref, right_ref):
        pooled_ref[:, :half] = ((0.25 / GELU_K) * dot(s_ref[...], left_ref[...], (1, 0)) + bias_ref[:, :half]).astype(BF16)
        pooled_ref[:, half:] = ((0.25 / GELU_K) * dot(s_ref[...], right_ref[:, :edge], (1, 0)) + bias_ref[:, half:]).astype(BF16)

    @pl.when(core_ref[0] == 0)
    def _():
        project(own_ref, other_ref)

    @pl.when(core_ref[0] != 0)
    def _():
        project(other_ref, own_ref)


VMEM = pl.BlockSpec(memory_space=pltpu.VMEM)
SMEM = pl.BlockSpec(memory_space=pltpu.SMEM)
TILE, CHUNK = 512, 32


def make_features(core, inner, bases, outer, cot, kw, shards):
    rows = bases.shape[1]
    return pl.pallas_call(
        functools.partial(feature_kernel, kw, TILE),
        out_shape=(jax.ShapeDtypeStruct((LANES, rows), BF16), jax.ShapeDtypeStruct((shards, LANES), F32)),
        in_specs=[SMEM] + [VMEM] * 4,
        out_specs=(VMEM, VMEM),
        scratch_shapes=[pltpu.VMEM((1, rows + 2 * LANES), F32), pltpu.VMEM((TILE, TILE), BF16)],
        compiler_params=pltpu.CompilerParams(vmem_limit_bytes=16 << 20),
        cost_estimate=pl.CostEstimate(flops=2 * LANES * TILE * rows, bytes_accessed=2 << 20, transcendentals=0),
        name="features",
    )(core, inner, bases, outer, cot)


def backward(core, feat, sums, own, other, cot, kw, shards):
    d0, half = own.shape
    pairs, d1 = cot.shape
    rows = 2 * pairs
    dims = (kw, shards, d0, d1, rows, TILE, CHUNK)
    return pl.pallas_call(
        functools.partial(step_kernel, dims),
        out_shape=(
            jax.ShapeDtypeStruct((d0, half), BF16),
            jax.ShapeDtypeStruct((pairs, d0), BF16),
            jax.ShapeDtypeStruct((d0, LANES), F32),
            jax.ShapeDtypeStruct((1, d1), F32),
        ),
        in_specs=[SMEM] + [VMEM] * 5,
        out_specs=(VMEM,) * 4,
        scratch_shapes=[
            pltpu.VMEM((d0, 2 * half), BF16),
            pltpu.VMEM((LANES, d0), BF16),
            pltpu.VMEM((rows, d0), BF16),
            pltpu.VMEM((pairs, d0), F32),
            pltpu.VMEM((rows, d0), BF16),
            pltpu.VMEM((LANES, d0), F32),
        ],
        compiler_params=pltpu.CompilerParams(vmem_limit_bytes=28 << 20),
        cost_estimate=pl.CostEstimate(flops=6 * pairs * d0 * d1, bytes_accessed=6 << 20, transcendentals=rows * d0),
        name="backward",
    )(core, feat, sums, own, other, cot)


def keep_half(core, s, cot, wide, half):
    pairs, d0 = s.shape
    return pl.pallas_call(
        keep_kernel,
        out_shape=jax.ShapeDtypeStruct((d0, half), F32),
        in_specs=[SMEM] + [VMEM] * 3,
        out_specs=VMEM,
        compiler_params=pltpu.CompilerParams(vmem_limit_bytes=16 << 20),
        cost_estimate=pl.CostEstimate(flops=2 * pairs * d0 * half, bytes_accessed=4 << 20, transcendentals=0),
        name="keep_half",
    )(core, s, cot, wide)


def pool(core, s, own, other, bias):
    pairs, d0 = s.shape
    d1 = bias.shape[1]
    return pl.pallas_call(
        pool_kernel,
        out_shape=jax.ShapeDtypeStruct((pairs, d1), BF16),
        in_specs=[SMEM] + [VMEM] * 4,
        out_specs=VMEM,
        compiler_params=pltpu.CompilerParams(vmem_limit_bytes=16 << 20),
        cost_estimate=pl.CostEstimate(flops=2 * pairs * d0 * d1, bytes_accessed=4 << 20, transcendentals=0),
        name="pool",
    )(core, s, own, other, bias)


def pack_kernel(core_ref, bases_hbm, embed_hbm, embed_bias_hbm, gain_hbm, proj_hbm, proj_bias_hbm,
                out_ref, inner_ref, outer_ref,
                bases_ref, embed_ref, embed_bias_ref, gain_ref, proj_ref, proj_bias_ref, rows_ref, block_ref, sems):
    kw, block, d1 = embed_ref.shape[0], proj_ref.shape[0], proj_ref.shape[1]
    copies, _, half = out_ref.shape
    taps, per = kw * 4, proj_bias_ref.shape[1]
    fetched = [
        pltpu.make_async_copy(source, target, sems.at[n])
        for n, (source, target) in enumerate((
            (bases_hbm, bases_ref), (embed_hbm, embed_ref), (embed_bias_hbm, embed_bias_ref),
            (gain_hbm, gain_ref), (proj_hbm, proj_ref), (proj_bias_hbm, proj_bias_ref)))
    ]
    for copy in fetched:
        copy.start()
    rows_ref[...] = jnp.zeros_like(rows_ref)
    for copy in fetched:
        copy.wait()
    first = bases_ref[:, :LANES] + 1
    last = bases_ref[:, bases_ref.shape[1] - LANES:] + 1
    even = core_ref[0] == 0
    inner_ref[...] = jnp.where(even, last, first)
    outer_ref[...] = jnp.where(even, first, last)
    for k in range(kw):
        rows_ref[4 * k:4 * k + 4, :block] = embed_ref[k].astype(F32)
    rows_ref[taps:taps + 1, :block] = embed_bias_ref[...].astype(F32)
    rows_ref[taps + 1:taps + 2, :block] = gain_ref[...].astype(F32)
    block_ref[...] = rows_ref[...].T[:block]
    block_ref[:1, 64:64 + per] = proj_bias_ref[...].astype(F32)
    edge = d1 - half

    @pl.when(even)
    def _():
        for i in range(copies):
            out_ref[i] = proj_ref[:, :half]

    @pl.when(jnp.logical_not(even))
    def _():
        for i in range(copies):
            out_ref[i, :, :edge] = proj_ref[:, half:]
            out_ref[i, :, edge:] = block_ref[...].astype(BF16)


def sum_kernel(scale, in_ref, out_ref):
    total = in_ref[0].astype(F32)
    for i in range(1, in_ref.shape[0]):
        total = total + in_ref[i].astype(F32)
    if scale != 1.0:
        total = total * scale
    total = total.astype(out_ref.dtype)
    for i in range(out_ref.shape[0]):
        out_ref[i] = total


def unpack_kernel(core_ref, total_ref, across_ref, embed_ref, embed_bias_ref, gain_ref, proj_ref, proj_bias_ref, rows_ref):
    kw, block, d1 = embed_ref.shape[0], proj_ref.shape[0], proj_ref.shape[1]
    half = total_ref.shape[1]
    taps, per, edge = kw * 4, proj_bias_ref.shape[1], d1 - half

    def place(left_ref, right_ref):
        proj_ref[:, :half] = left_ref[...]
        proj_ref[:, half:] = right_ref[:, :edge]
        rows_ref[:block, :] = right_ref[:, edge:]

    @pl.when(core_ref[0] == 0)
    def _():
        place(total_ref, across_ref)

    @pl.when(core_ref[0] != 0)
    def _():
        place(across_ref, total_ref)

    proj_bias_ref[...] = rows_ref[:1, 64:64 + per]
    rows_ref[block:, :] = jnp.zeros((LANES - block, LANES), F32)
    rows_ref[...] = rows_ref[...].T
    for k in range(kw):
        embed_ref[k] = rows_ref[4 * k:4 * k + 4, :block]
    embed_bias_ref[...] = rows_ref[taps:taps + 1, :block]
    gain_ref[...] = rows_ref[taps + 1:taps + 2, :block]


def local(bases, embed_weight, embed_bias, norm_gain, proj_weight, proj_bias, cotangent):
    kw = embed_weight.shape[0]
    shards, members = lax.axis_size("dp"), lax.axis_size("seq")
    block, d1 = proj_weight.shape
    per = proj_bias.shape[0]
    half = (d1 + LANES) // 2
    core = (lax.axis_index("seq") & 1).astype(jnp.int32).reshape(1)
    swap = [(i, i ^ 1) for i in range(members)]

    facing = [(i, i + 1 if i % 2 else i - 1) for i in range(1, members - 1)]

    hbm = pl.BlockSpec(memory_space=pltpu.HBM)
    gathered = (bases, embed_weight, embed_bias[None], norm_gain[None], proj_weight, proj_bias[None])
    piece, inner, outer = pl.pallas_call(
        pack_kernel,
        out_shape=(
            jax.ShapeDtypeStruct((shards, block, half), BF16),
            jax.ShapeDtypeStruct((1, LANES), jnp.int32),
            jax.ShapeDtypeStruct((1, LANES), jnp.int32),
        ),
        in_specs=[SMEM] + [hbm] * 6,
        out_specs=(VMEM,) * 3,
        scratch_shapes=[pltpu.VMEM(x.shape, x.dtype) for x in gathered] + [
            pltpu.VMEM((LANES, LANES), F32), pltpu.VMEM((block, LANES), F32), pltpu.SemaphoreType.DMA((6,))],
        compiler_params=pltpu.CompilerParams(vmem_limit_bytes=60 << 20),
        name="pack",
    )(core, *gathered)
    inner = lax.ppermute(inner, "seq", swap)
    outer = lax.ppermute(outer, "seq", facing)
    own = lax.all_to_all(piece, "dp", 0, 0, tiled=True).reshape(shards * block, half)
    feat, sums = make_features(core, inner, bases, outer, cotangent[0], kw, shards)
    own, feat, sums = lax.optimization_barrier((own, feat, sums))
    other = lax.ppermute(own, "seq", swap)

    cot = cotangent[0]
    theirs, s, wide, bias = backward(core, feat, sums, own, other, cot, kw, shards)
    came = lax.ppermute(theirs, "seq", swap)
    mine = keep_half(core, s, cot, wide, half)
    pooled = pool(core, s, own, other, bias)
    summed = (mine + came.astype(F32)).astype(BF16).reshape(shards, block, half)
    parts = lax.all_to_all(summed, "dp", 0, 0, tiled=True)
    parts, pooled = lax.optimization_barrier((parts, pooled))

    def add_up(parts, scale, copies, kind):
        return pl.pallas_call(
            functools.partial(sum_kernel, scale),
            out_shape=jax.ShapeDtypeStruct((copies, block, half), kind),
            in_specs=[VMEM],
            out_specs=VMEM,
            compiler_params=pltpu.CompilerParams(vmem_limit_bytes=4 << 20),
            name="add_up",
        )(parts)

    groups = [[i for i in range(members) if i % 2 == c] for c in range(2)]
    spread = lax.all_to_all(add_up(parts, 1.0, members // 2, BF16), "seq", 0, 0, axis_index_groups=groups, tiled=True)
    total = add_up(spread, 0.125 / (cotangent.shape[1] * members * shards), 1, F32)[0]
    across = lax.ppermute(total, "seq", swap)
    grad_embed, grad_embed_bias, grad_gain, grad_proj, grad_proj_bias = pl.pallas_call(
        unpack_kernel,
        out_shape=(
            jax.ShapeDtypeStruct(embed_weight.shape, F32),
            jax.ShapeDtypeStruct((1, block), F32),
            jax.ShapeDtypeStruct((1, block), F32),
            jax.ShapeDtypeStruct((block, d1), F32),
            jax.ShapeDtypeStruct((1, per), F32),
        ),
        in_specs=[SMEM, VMEM, VMEM],
        out_specs=(VMEM,) * 5,
        scratch_shapes=[pltpu.VMEM((LANES, LANES), F32)],
        compiler_params=pltpu.CompilerParams(vmem_limit_bytes=4 << 20),
        name="unpack",
    )(core, total, across)
    return (pooled[None], grad_embed, grad_embed_bias[0], grad_gain[0], grad_proj, grad_proj_bias[0])


def solution(mesh):
    placed = (
        P("dp", "seq"),
        P(None, None, "dp"),
        P("dp"),
        P("dp"),
        P("dp", None),
        P("dp"),
        P("dp", "seq", None),
    )
    return jax.shard_map(
        local,
        mesh=mesh,
        in_specs=placed,
        out_specs=(
            P("dp", "seq", None),
            P(None, None, "dp"),
            P("dp"),
            P("dp"),
            P("dp", None),
            P("dp"),
        ),
        check_vma=False,
    )
```

```python
import functools

import jax
import jax.numpy as jnp
from jax import lax
from jax.experimental import pallas as pl
from jax.experimental.pallas import tpu as pltpu
from jax.sharding import PartitionSpec as P

F32, BF16 = jnp.float32, jnp.bfloat16
LANES = 128
GELU_A = 0.7978845608028654
GELU_B = 0.044715
GELU_K = (GELU_A * GELU_B) ** (1 / 3)
GELU_C = GELU_A / GELU_K
EPSILON = 1e-06


def dot(a, b, contract, precision=None):
    return lax.dot_general(a, b, ((contract[:1], contract[1:]), ((), ())), precision=precision, preferred_element_type=F32)


def iota(shape, dim):
    return lax.broadcasted_iota(jnp.int32, shape, dim)


def by_owner(shards, d1):
    per = d1 // shards
    column = iota((LANES, d1), 1)
    owner = (column * 2341) >> 16
    spread = (iota((LANES, d1), 0) == column - owner * per + 64).astype(F32)
    return owner[:shards] == iota((shards, d1), 0), spread


def feature_kernel(kw, tile, core_ref, inner_ref, bases_ref, outer_ref, cot_ref, feat_ref, sums_ref, code_ref, perm_ref):
    rows = bases_ref.shape[1]
    pair_tile, reach, taps = tile // 2, kw // 2, kw * 4

    @pl.when(core_ref[0] == 0)
    def _():
        code_ref[:, :LANES] = outer_ref[...].astype(F32)
        code_ref[:, LANES + rows:] = inner_ref[...].astype(F32)

    @pl.when(core_ref[0] != 0)
    def _():
        code_ref[:, :LANES] = inner_ref[...].astype(F32)
        code_ref[:, LANES + rows:] = outer_ref[...].astype(F32)

    code_ref[:, LANES:LANES + rows] = (bases_ref[...] + 1).astype(F32)
    source, place = iota((tile, tile), 0), iota((tile, tile), 1)
    perm_ref[...] = (source == jnp.where(place < pair_tile, 2 * place, 2 * (place - pair_tile) + 1)).astype(BF16)
    repeat = ((iota((LANES, 16), 0) >> 2) == iota((LANES, 16), 1)).astype(BF16)
    letter = (iota((LANES, tile), 0) & 3) + 1
    line = iota((LANES, tile), 0)
    for t in range(rows // tile):
        window = code_ref[:, t * tile:t * tile + tile + 2 * LANES]
        start = LANES - reach
        shifted = jnp.concatenate([window[:, start + k:start + k + tile] for k in range(kw)] + [jnp.zeros((1, tile), F32)], axis=0)
        spreaded = dot(repeat, shifted.astype(BF16), (1, 0))
        hot = ((spreaded == letter.astype(F32)) & (line < taps)) | (line == taps)
        ordered = dot(hot.astype(F32).astype(BF16), perm_ref[...], (1, 0))
        feat_ref[:, t * tile:(t + 1) * tile] = ordered.astype(BF16)

    shards = sums_ref.shape[0]
    owned, spread = by_owner(shards, cot_ref.shape[1])
    sums = 4.0 * jnp.sum(cot_ref[...].astype(F32), axis=0, keepdims=True)
    sums_ref[...] = dot(jnp.where(owned, sums, 0.0), spread, (1, 1), lax.Precision.HIGHEST)


def step_kernel(dims, core_ref, feat_ref, sums_ref, own_ref, other_ref, cot_ref,
                theirs_ref, s_ref, wide_ref, bias_ref, w_ref,
                we_ref, emb_ref, ga_ref, ge_ref, gew_ref):
    kw, shards, d0, d1, rows, tile, chunk = dims
    half = w_ref.shape[1] // 2
    pair_tile = tile // 2
    taps = kw * 4
    core = core_ref[0]
    block = d0 // shards

    @pl.when(core == 0)
    def _():
        w_ref[:, :half] = own_ref[...]
        w_ref[:, half:] = other_ref[...]

    @pl.when(core != 0)
    def _():
        w_ref[:, :half] = other_ref[...]
        w_ref[:, half:] = own_ref[...]

    wide = w_ref[:, d1:].astype(F32)
    wide_ref[...] = wide
    we_ref[...] = wide.T.astype(BF16)
    gain = we_ref[pl.ds(64 - 8, 8), :].astype(F32)[5:6, :]
    gain_y = gain * GELU_K

    owned, spread = by_owner(shards, d1)
    pieces = wide_ref[pl.ds(0, shards, stride=block), :]
    bias_ref[...] = jnp.sum(jnp.where(owned, dot(pieces.astype(BF16), spread.astype(BF16), (1, 0)), 0.0), axis=0, keepdims=True)

    for t in range(rows // tile):
        at = t * tile
        emb_ref[at:at + tile, :] = dot(feat_ref[:, at:at + tile], we_ref[...], (0, 0)).astype(BF16)
        half_at = t * pair_tile
        ga_ref[half_at:half_at + pair_tile, :] = dot(cot_ref[half_at:half_at + pair_tile, :], w_ref[:, :d1], (1, 1))

        def side(start, grad):
            values = emb_ref[pl.ds(start, chunk), :].astype(F32)
            inverse = lax.rsqrt(jnp.sum(values * values, axis=1, keepdims=True) * (1.0 / d0) + EPSILON)
            y = (values * inverse) * gain_y
            square = y * y
            tanh = jnp.tanh(y * (GELU_C + square))
            above, below = 1.0 + tanh, 1.0 - tanh
            activated = y * above
            slope = above + (activated * below) * (GELU_C + 3.0 * square)
            grad_normed = grad * slope
            toward_gain = grad_normed * y
            shared = jnp.sum(toward_gain, axis=1, keepdims=True) * (inverse * inverse * (1.0 / (GELU_K * d0)))
            ge_ref[pl.ds(start, chunk), :] = (inverse * (grad_normed * gain) - values * shared).astype(BF16)
            return activated, toward_gain

        def body(i, total):
            first = pl.multiple_of(at + i * chunk, chunk)
            second = pl.multiple_of(at + pair_tile + i * chunk, chunk)
            pair_at = pl.multiple_of(half_at + i * chunk, chunk)
            grad = ga_ref[pl.ds(pair_at, chunk), :]
            act_even, gain_even = side(first, grad)
            act_odd, gain_odd = side(second, grad)
            s_ref[pl.ds(pair_at, chunk), :] = (act_even + act_odd).astype(BF16)
            both = gain_even + gain_odd
            for r in range(0, chunk, 8):
                total = total + both[r:r + 8]
            return total

        start_total = jnp.zeros((8, d0), F32)
        gain_total = lax.fori_loop(0, pair_tile // chunk, body, start_total, unroll=True)
        part = dot(feat_ref[:, at:at + tile], ge_ref[at:at + tile, :], (1, 0))
        is_gain = iota((LANES, d0), 0) == taps + 1
        part = jnp.where(is_gain, jnp.sum(gain_total, axis=0, keepdims=True) / gain_y, part)
        if t == 0:
            gew_ref[...] = part
        else:
            gew_ref[...] += part

    wide_ref[...] = gew_ref[...].T
    wide_ref[pl.ds(0, shards, stride=block), :] = wide_ref[pl.ds(0, shards, stride=block), :] + sums_ref[...]

    @pl.when(core == 0)
    def _():
        right_half(s_ref, cot_ref, wide_ref, theirs_ref)

    @pl.when(core != 0)
    def _():
        left_half(s_ref, cot_ref, theirs_ref)


def left_half(s_ref, cot_ref, out_ref):
    half = out_ref.shape[1]
    out_ref[...] = (dot(s_ref[...], cot_ref[:, :half], (0, 0)) * (1.0 / GELU_K)).astype(out_ref.dtype)


def right_half(s_ref, cot_ref, wide_ref, out_ref):
    half = out_ref.shape[1]
    edge = cot_ref.shape[1] - half
    out_ref[:, :edge] = (dot(s_ref[...], cot_ref[:, half:], (0, 0)) * (1.0 / GELU_K)).astype(out_ref.dtype)
    out_ref[:, edge:] = wide_ref[...].astype(out_ref.dtype)


def keep_kernel(core_ref, s_ref, cot_ref, wide_ref, mine_ref):
    @pl.when(core_ref[0] == 0)
    def _():
        left_half(s_ref, cot_ref, mine_ref)

    @pl.when(core_ref[0] != 0)
    def _():
        right_half(s_ref, cot_ref, wide_ref, mine_ref)


def pool_kernel(s_ref, w_ref, bias_ref, pooled_hbm, stage_ref, sems):
    parts, step, d1 = stage_ref.shape
    copies = [pltpu.make_async_copy(stage_ref.at[n], pooled_hbm.at[pl.ds(n * step, step), :], sems.at[n]) for n in range(parts)]
    for n in range(parts):
        mixed = dot(s_ref[n * step:(n + 1) * step, :], w_ref[:, :d1], (1, 0))
        stage_ref[n] = ((0.25 / GELU_K) * mixed + bias_ref[...]).astype(BF16)
        copies[n].start()
    for copy in copies:
        copy.wait()


VMEM = pl.BlockSpec(memory_space=pltpu.VMEM)
SMEM = pl.BlockSpec(memory_space=pltpu.SMEM)
TILE, CHUNK = 1536, 32


def make_features(core, inner, bases, outer, cot, kw, shards):
    rows = bases.shape[1]
    return pl.pallas_call(
        functools.partial(feature_kernel, kw, TILE),
        out_shape=(jax.ShapeDtypeStruct((LANES, rows), BF16), jax.ShapeDtypeStruct((shards, LANES), F32)),
        in_specs=[SMEM] + [VMEM] * 4,
        out_specs=(VMEM, VMEM),
        scratch_shapes=[pltpu.VMEM((1, rows + 2 * LANES), F32), pltpu.VMEM((TILE, TILE), BF16)],
        compiler_params=pltpu.CompilerParams(vmem_limit_bytes=16 << 20),
        cost_estimate=pl.CostEstimate(flops=2 * LANES * TILE * rows, bytes_accessed=2 << 20, transcendentals=0),
        name="features",
    )(core, inner, bases, outer, cot)


def backward(core, feat, sums, own, other, cot, kw, shards):
    d0, half = own.shape
    pairs, d1 = cot.shape
    rows = 2 * pairs
    dims = (kw, shards, d0, d1, rows, TILE, CHUNK)
    return pl.pallas_call(
        functools.partial(step_kernel, dims),
        out_shape=(
            jax.ShapeDtypeStruct((d0, half), BF16),
            jax.ShapeDtypeStruct((pairs, d0), BF16),
            jax.ShapeDtypeStruct((d0, LANES), F32),
            jax.ShapeDtypeStruct((1, d1), F32),
            jax.ShapeDtypeStruct((d0, 2 * half), BF16),
        ),
        in_specs=[SMEM] + [VMEM] * 5,
        out_specs=(VMEM,) * 5,
        scratch_shapes=[
            pltpu.VMEM((LANES, d0), BF16),
            pltpu.VMEM((rows, d0), BF16),
            pltpu.VMEM((pairs, d0), F32),
            pltpu.VMEM((rows, d0), BF16),
            pltpu.VMEM((LANES, d0), F32),
        ],
        compiler_params=pltpu.CompilerParams(vmem_limit_bytes=28 << 20),
        cost_estimate=pl.CostEstimate(flops=6 * pairs * d0 * d1, bytes_accessed=6 << 20, transcendentals=rows * d0),
        name="backward",
    )(core, feat, sums, own, other, cot)


def keep_half(core, s, cot, wide, half):
    pairs, d0 = s.shape
    return pl.pallas_call(
        keep_kernel,
        out_shape=jax.ShapeDtypeStruct((d0, half), F32),
        in_specs=[SMEM] + [VMEM] * 3,
        out_specs=VMEM,
        compiler_params=pltpu.CompilerParams(vmem_limit_bytes=16 << 20),
        cost_estimate=pl.CostEstimate(flops=2 * pairs * d0 * half, bytes_accessed=4 << 20, transcendentals=0),
        name="keep_half",
    )(core, s, cot, wide)


def pool(s, w, bias):
    pairs, d0 = s.shape
    d1 = bias.shape[1]
    hbm = pl.BlockSpec(memory_space=pltpu.HBM)
    parts = 3
    return pl.pallas_call(
        pool_kernel,
        out_shape=jax.ShapeDtypeStruct((pairs, d1), BF16),
        in_specs=[VMEM] * 3,
        out_specs=hbm,
        scratch_shapes=[pltpu.VMEM((parts, pairs // parts, d1), BF16), pltpu.SemaphoreType.DMA((parts,))],
        compiler_params=pltpu.CompilerParams(vmem_limit_bytes=16 << 20),
        cost_estimate=pl.CostEstimate(flops=2 * pairs * d0 * d1, bytes_accessed=4 << 20, transcendentals=0),
        name="pool",
    )(s, w, bias)


def pack_kernel(core_ref, bases_hbm, embed_hbm, embed_bias_hbm, gain_hbm, proj_hbm, proj_bias_hbm,
                out_hbm, inner_ref, outer_ref,
                bases_ref, embed_ref, embed_bias_ref, gain_ref, proj_ref, proj_bias_ref, rows_ref, stage_ref, sems, sent):
    kw, block, d1 = embed_ref.shape[0], proj_ref.shape[0], proj_ref.shape[1]
    copies, _, half = out_hbm.shape
    taps, per = kw * 4, proj_bias_ref.shape[1]
    fetched = [
        pltpu.make_async_copy(source, target, sems.at[n])
        for n, (source, target) in enumerate((
            (bases_hbm, bases_ref), (embed_hbm, embed_ref), (embed_bias_hbm, embed_bias_ref),
            (gain_hbm, gain_ref), (proj_hbm, proj_ref), (proj_bias_hbm, proj_bias_ref)))
    ]
    for copy in fetched:
        copy.start()
    rows_ref[...] = jnp.zeros_like(rows_ref)
    for copy in fetched:
        copy.wait()
    even = core_ref[0] == 0
    edge = d1 - half

    @pl.when(even)
    def _():
        stage_ref[...] = proj_ref[:, :half]

    @pl.when(jnp.logical_not(even))
    def _():
        for k in range(kw):
            rows_ref[4 * k:4 * k + 4, :block] = embed_ref[k].astype(F32)
        rows_ref[taps:taps + 1, :block] = embed_bias_ref[...].astype(F32)
        rows_ref[taps + 1:taps + 2, :block] = gain_ref[...].astype(F32)
        rows_ref[...] = rows_ref[...].T
        rows_ref[:1, 64:64 + per] = proj_bias_ref[...].astype(F32)
        stage_ref[:, :edge] = proj_ref[:, half:]
        stage_ref[:, edge:] = rows_ref[:block, :].astype(BF16)

    sends = [pltpu.make_async_copy(stage_ref, out_hbm.at[i], sent.at[i]) for i in range(copies)]
    for send in sends:
        send.start()
    first = bases_ref[:, :LANES] + 1
    last = bases_ref[:, bases_ref.shape[1] - LANES:] + 1
    inner_ref[...] = jnp.where(even, last, first)
    outer_ref[...] = jnp.where(even, first, last)
    for send in sends:
        send.wait()


def sum_kernel(scale, in_ref, out_ref):
    total = in_ref[0].astype(F32)
    for i in range(1, in_ref.shape[0]):
        total = total + in_ref[i].astype(F32)
    if scale != 1.0:
        total = total * scale
    total = total.astype(out_ref.dtype)
    for i in range(out_ref.shape[0]):
        out_ref[i] = total


def unpack_kernel(core_ref, total_ref, across_ref, embed_ref, embed_bias_ref, gain_ref, proj_ref, proj_bias_ref, rows_ref):
    kw, block, d1 = embed_ref.shape[0], proj_ref.shape[0], proj_ref.shape[1]
    half = total_ref.shape[1]
    taps, per, edge = kw * 4, proj_bias_ref.shape[1], d1 - half

    def place(left_ref, right_ref):
        proj_ref[:, :half] = left_ref[...]
        proj_ref[:, half:] = right_ref[:, :edge]
        rows_ref[:block, :] = right_ref[:, edge:]

    @pl.when(core_ref[0] == 0)
    def _():
        place(total_ref, across_ref)

    @pl.when(core_ref[0] != 0)
    def _():
        place(across_ref, total_ref)

    proj_bias_ref[...] = rows_ref[:1, 64:64 + per]
    rows_ref[block:, :] = jnp.zeros((LANES - block, LANES), F32)
    rows_ref[...] = rows_ref[...].T
    for k in range(kw):
        embed_ref[k] = rows_ref[4 * k:4 * k + 4, :block]
    embed_bias_ref[...] = rows_ref[taps:taps + 1, :block]
    gain_ref[...] = rows_ref[taps + 1:taps + 2, :block]


def local(bases, embed_weight, embed_bias, norm_gain, proj_weight, proj_bias, cotangent):
    kw = embed_weight.shape[0]
    shards, members = lax.axis_size("dp"), lax.axis_size("seq")
    block, d1 = proj_weight.shape
    per = proj_bias.shape[0]
    half = (d1 + LANES) // 2
    core = (lax.axis_index("seq") & 1).astype(jnp.int32).reshape(1)
    swap = [(i, i ^ 1) for i in range(members)]

    facing = [(i, i + 1 if i % 2 else i - 1) for i in range(1, members - 1)]

    hbm = pl.BlockSpec(memory_space=pltpu.HBM)
    gathered = (bases, embed_weight, embed_bias[None], norm_gain[None], proj_weight, proj_bias[None])
    piece, inner, outer = pl.pallas_call(
        pack_kernel,
        out_shape=(
            jax.ShapeDtypeStruct((shards, block, half), BF16),
            jax.ShapeDtypeStruct((1, LANES), jnp.int32),
            jax.ShapeDtypeStruct((1, LANES), jnp.int32),
        ),
        in_specs=[SMEM] + [hbm] * 6,
        out_specs=(hbm, VMEM, VMEM),
        scratch_shapes=[pltpu.VMEM(x.shape, x.dtype) for x in gathered] + [
            pltpu.VMEM((LANES, LANES), F32), pltpu.VMEM((block, half), BF16),
            pltpu.SemaphoreType.DMA((6,)), pltpu.SemaphoreType.DMA((shards,))],
        compiler_params=pltpu.CompilerParams(vmem_limit_bytes=60 << 20),
        name="pack",
    )(core, *gathered)
    inner = lax.ppermute(inner, "seq", swap)
    outer = lax.ppermute(outer, "seq", facing)
    own = lax.all_to_all(piece, "dp", 0, 0, tiled=True).reshape(shards * block, half)
    feat, sums = make_features(core, inner, bases, outer, cotangent[0], kw, shards)
    own, feat, sums = lax.optimization_barrier((own, feat, sums))
    other = lax.ppermute(own, "seq", swap)

    cot = cotangent[0]
    theirs, s, wide, bias, w = backward(core, feat, sums, own, other, cot, kw, shards)
    came = lax.ppermute(theirs, "seq", swap)
    mine = keep_half(core, s, cot, wide, half)
    pooled = pool(s, w, bias)
    summed = (mine + came.astype(F32)).astype(BF16).reshape(shards, block, half)
    parts = lax.all_to_all(summed, "dp", 0, 0, tiled=True)

    def add_up(parts, scale, copies, kind):
        return pl.pallas_call(
            functools.partial(sum_kernel, scale),
            out_shape=jax.ShapeDtypeStruct((copies, block, half), kind),
            in_specs=[VMEM],
            out_specs=VMEM,
            compiler_params=pltpu.CompilerParams(vmem_limit_bytes=4 << 20),
            name="add_up",
        )(parts)

    groups = [[i for i in range(members) if i % 2 == c] for c in range(2)]
    spread = lax.all_to_all(add_up(parts, 1.0, members // 2, BF16), "seq", 0, 0, axis_index_groups=groups, tiled=True)
    total = add_up(spread, 0.125 / (cotangent.shape[1] * members * shards), 1, F32)[0]
    across = lax.ppermute(total, "seq", swap)
    grad_embed, grad_embed_bias, grad_gain, grad_proj, grad_proj_bias = pl.pallas_call(
        unpack_kernel,
        out_shape=(
            jax.ShapeDtypeStruct(embed_weight.shape, F32),
            jax.ShapeDtypeStruct((1, block), F32),
            jax.ShapeDtypeStruct((1, block), F32),
            jax.ShapeDtypeStruct((block, d1), F32),
            jax.ShapeDtypeStruct((1, per), F32),
        ),
        in_specs=[SMEM, VMEM, VMEM],
        out_specs=(VMEM,) * 5,
        scratch_shapes=[pltpu.VMEM((LANES, LANES), F32)],
        compiler_params=pltpu.CompilerParams(vmem_limit_bytes=4 << 20),
        name="unpack",
    )(core, total, across)
    return (pooled[None], grad_embed, grad_embed_bias[0], grad_gain[0], grad_proj, grad_proj_bias[0])


def solution(mesh):
    placed = (
        P("dp", "seq"),
        P(None, None, "dp"),
        P("dp"),
        P("dp"),
        P("dp", None),
        P("dp"),
        P("dp", "seq", None),
    )
    return jax.shard_map(
        local,
        mesh=mesh,
        in_specs=placed,
        out_specs=(
            P("dp", "seq", None),
            P(None, None, "dp"),
            P("dp"),
            P("dp"),
            P("dp", None),
            P("dp"),
        ),
        check_vma=False,
    )
```

```python
import functools

import jax
import jax.numpy as jnp
from jax import lax
from jax.experimental import pallas as pl
from jax.experimental.pallas import tpu as pltpu
from jax.sharding import PartitionSpec as P

F32, BF16 = jnp.float32, jnp.bfloat16
LANES = 128
GELU_A = 0.7978845608028654
GELU_B = 0.044715
GELU_K = (GELU_A * GELU_B) ** (1 / 3)
GELU_C = GELU_A / GELU_K
EPSILON = 1e-06


def dot(a, b, contract, precision=None):
    return lax.dot_general(a, b, ((contract[:1], contract[1:]), ((), ())), precision=precision, preferred_element_type=F32)


def iota(shape, dim):
    return lax.broadcasted_iota(jnp.int32, shape, dim)


def by_owner(shards, d1):
    per = d1 // shards
    column = iota((LANES, d1), 1)
    owner = (column * 2341) >> 16
    spread = (iota((LANES, d1), 0) == column - owner * per + 64).astype(F32)
    return owner[:shards] == iota((shards, d1), 0), spread


def feature_kernel(kw, tile, core_ref, inner_ref, bases_ref, outer_ref, cot_ref, feat_ref, sums_ref, code_ref, perm_ref):
    rows = bases_ref.shape[1]
    pair_tile, reach, taps = tile // 2, kw // 2, kw * 4

    @pl.when(core_ref[0] == 0)
    def _():
        code_ref[:, :LANES] = outer_ref[...].astype(F32)
        code_ref[:, LANES + rows:] = inner_ref[...].astype(F32)

    @pl.when(core_ref[0] != 0)
    def _():
        code_ref[:, :LANES] = inner_ref[...].astype(F32)
        code_ref[:, LANES + rows:] = outer_ref[...].astype(F32)

    code_ref[:, LANES:LANES + rows] = (bases_ref[...] + 1).astype(F32)
    source, place = iota((tile, tile), 0), iota((tile, tile), 1)
    perm_ref[...] = (source == jnp.where(place < pair_tile, 2 * place, 2 * (place - pair_tile) + 1)).astype(BF16)
    repeat = ((iota((LANES, 16), 0) >> 2) == iota((LANES, 16), 1)).astype(BF16)
    letter = (iota((LANES, tile), 0) & 3) + 1
    line = iota((LANES, tile), 0)
    for t in range(rows // tile):
        window = code_ref[:, t * tile:t * tile + tile + 2 * LANES]
        start = LANES - reach
        shifted = jnp.concatenate([window[:, start + k:start + k + tile] for k in range(kw)] + [jnp.zeros((1, tile), F32)], axis=0)
        spreaded = dot(repeat, shifted.astype(BF16), (1, 0))
        hot = ((spreaded == letter.astype(F32)) & (line < taps)) | (line == taps)
        ordered = dot(hot.astype(F32).astype(BF16), perm_ref[...], (1, 0))
        feat_ref[:, t * tile:(t + 1) * tile] = ordered.astype(BF16)

    shards = sums_ref.shape[0]
    owned, spread = by_owner(shards, cot_ref.shape[1])
    sums = 4.0 * jnp.sum(cot_ref[...].astype(F32), axis=0, keepdims=True)
    sums_ref[...] = dot(jnp.where(owned, sums, 0.0), spread, (1, 1), lax.Precision.HIGHEST)


def step_kernel(dims, core_ref, feat_ref, sums_ref, own_ref, other_ref, cot_ref,
                theirs_ref, s_ref, wide_ref, bias_ref, w_ref,
                we_ref, emb_ref, ga_ref, ge_ref, gew_ref):
    kw, shards, d0, d1, rows, tile, chunk = dims
    half = w_ref.shape[1] // 2
    pair_tile = tile // 2
    taps = kw * 4
    core = core_ref[0]
    block = d0 // shards

    @pl.when(core == 0)
    def _():
        w_ref[:, :half] = own_ref[...]
        w_ref[:, half:] = other_ref[...]

    @pl.when(core != 0)
    def _():
        w_ref[:, :half] = other_ref[...]
        w_ref[:, half:] = own_ref[...]

    wide = w_ref[:, d1:].astype(F32)
    wide_ref[...] = wide
    we_ref[...] = wide.T.astype(BF16)
    gain = we_ref[pl.ds(64 - 8, 8), :].astype(F32)[5:6, :]
    gain_y = gain * GELU_K

    owned, spread = by_owner(shards, d1)
    pieces = wide_ref[pl.ds(0, shards, stride=block), :]
    bias_ref[...] = jnp.sum(jnp.where(owned, dot(pieces.astype(BF16), spread.astype(BF16), (1, 0)), 0.0), axis=0, keepdims=True)

    for t in range(rows // tile):
        at = t * tile
        emb_ref[at:at + tile, :] = dot(feat_ref[:, at:at + tile], we_ref[...], (0, 0)).astype(BF16)
        half_at = t * pair_tile
        ga_ref[half_at:half_at + pair_tile, :] = dot(cot_ref[half_at:half_at + pair_tile, :], w_ref[:, :d1], (1, 1))

        def side(start, grad):
            values = emb_ref[pl.ds(start, chunk), :].astype(F32)
            inverse = lax.rsqrt(jnp.sum(values * values, axis=1, keepdims=True) * (1.0 / d0) + EPSILON)
            y = (values * inverse) * gain_y
            square = y * y
            tanh = jnp.tanh(y * (GELU_C + square))
            above, below = 1.0 + tanh, 1.0 - tanh
            activated = y * above
            slope = above + (activated * below) * (GELU_C + 3.0 * square)
            grad_normed = grad * slope
            toward_gain = grad_normed * y
            shared = jnp.sum(toward_gain, axis=1, keepdims=True) * (inverse * inverse * (1.0 / (GELU_K * d0)))
            ge_ref[pl.ds(start, chunk), :] = (inverse * (grad_normed * gain) - values * shared).astype(BF16)
            return activated, toward_gain

        def body(i, total):
            first = pl.multiple_of(at + i * chunk, chunk)
            second = pl.multiple_of(at + pair_tile + i * chunk, chunk)
            pair_at = pl.multiple_of(half_at + i * chunk, chunk)
            grad = ga_ref[pl.ds(pair_at, chunk), :]
            act_even, gain_even = side(first, grad)
            act_odd, gain_odd = side(second, grad)
            s_ref[pl.ds(pair_at, chunk), :] = (act_even + act_odd).astype(BF16)
            both = gain_even + gain_odd
            for r in range(0, chunk, 8):
                total = total + both[r:r + 8]
            return total

        start_total = jnp.zeros((8, d0), F32)
        gain_total = lax.fori_loop(0, pair_tile // chunk, body, start_total, unroll=True)
        part = dot(feat_ref[:, at:at + tile], ge_ref[at:at + tile, :], (1, 0))
        is_gain = iota((LANES, d0), 0) == taps + 1
        part = jnp.where(is_gain, jnp.sum(gain_total, axis=0, keepdims=True) / gain_y, part)
        if t == 0:
            gew_ref[...] = part
        else:
            gew_ref[...] += part

    wide_ref[...] = gew_ref[...].T
    wide_ref[pl.ds(0, shards, stride=block), :] = wide_ref[pl.ds(0, shards, stride=block), :] + sums_ref[...]

    @pl.when(core == 0)
    def _():
        right_half(s_ref, cot_ref, wide_ref, theirs_ref)

    @pl.when(core != 0)
    def _():
        left_half(s_ref, cot_ref, theirs_ref)


def left_half(s_ref, cot_ref, out_ref):
    half = out_ref.shape[1]
    out_ref[...] = (dot(s_ref[...], cot_ref[:, :half], (0, 0)) * (1.0 / GELU_K)).astype(out_ref.dtype)


def right_half(s_ref, cot_ref, wide_ref, out_ref):
    half = out_ref.shape[1]
    edge = cot_ref.shape[1] - half
    out_ref[:, :edge] = (dot(s_ref[...], cot_ref[:, half:], (0, 0)) * (1.0 / GELU_K)).astype(out_ref.dtype)
    out_ref[:, edge:] = wide_ref[...].astype(out_ref.dtype)


def keep_kernel(core_ref, s_ref, cot_ref, wide_ref, mine_ref):
    @pl.when(core_ref[0] == 0)
    def _():
        left_half(s_ref, cot_ref, mine_ref)

    @pl.when(core_ref[0] != 0)
    def _():
        right_half(s_ref, cot_ref, wide_ref, mine_ref)


def pool_kernel(s_ref, w_ref, bias_ref, pooled_hbm, stage_ref, sems):
    parts, step, d1 = stage_ref.shape
    copies = [pltpu.make_async_copy(stage_ref.at[n], pooled_hbm.at[pl.ds(n * step, step), :], sems.at[n]) for n in range(parts)]
    for n in range(parts):
        mixed = dot(s_ref[n * step:(n + 1) * step, :], w_ref[:, :d1], (1, 0))
        stage_ref[n] = ((0.25 / GELU_K) * mixed + bias_ref[...]).astype(BF16)
        copies[n].start()
    for copy in copies:
        copy.wait()


VMEM = pl.BlockSpec(memory_space=pltpu.VMEM)
SMEM = pl.BlockSpec(memory_space=pltpu.SMEM)
TILE, CHUNK = 1536, 32


def make_features(core, inner, bases, outer, cot, kw, shards):
    rows = bases.shape[1]
    return pl.pallas_call(
        functools.partial(feature_kernel, kw, TILE),
        out_shape=(jax.ShapeDtypeStruct((LANES, rows), BF16), jax.ShapeDtypeStruct((shards, LANES), F32)),
        in_specs=[SMEM] + [VMEM] * 4,
        out_specs=(VMEM, VMEM),
        scratch_shapes=[pltpu.VMEM((1, rows + 2 * LANES), F32), pltpu.VMEM((TILE, TILE), BF16)],
        compiler_params=pltpu.CompilerParams(vmem_limit_bytes=16 << 20),
        cost_estimate=pl.CostEstimate(flops=2 * LANES * TILE * rows, bytes_accessed=2 << 20, transcendentals=0),
        name="features",
    )(core, inner, bases, outer, cot)


def backward(core, feat, sums, own, other, cot, kw, shards):
    d0, half = own.shape
    pairs, d1 = cot.shape
    rows = 2 * pairs
    dims = (kw, shards, d0, d1, rows, TILE, CHUNK)
    return pl.pallas_call(
        functools.partial(step_kernel, dims),
        out_shape=(
            jax.ShapeDtypeStruct((d0, half), BF16),
            jax.ShapeDtypeStruct((pairs, d0), BF16),
            jax.ShapeDtypeStruct((d0, LANES), F32),
            jax.ShapeDtypeStruct((1, d1), F32),
            jax.ShapeDtypeStruct((d0, 2 * half), BF16),
        ),
        in_specs=[SMEM] + [VMEM] * 5,
        out_specs=(VMEM,) * 5,
        scratch_shapes=[
            pltpu.VMEM((LANES, d0), BF16),
            pltpu.VMEM((rows, d0), BF16),
            pltpu.VMEM((pairs, d0), F32),
            pltpu.VMEM((rows, d0), BF16),
            pltpu.VMEM((LANES, d0), F32),
        ],
        compiler_params=pltpu.CompilerParams(vmem_limit_bytes=28 << 20),
        cost_estimate=pl.CostEstimate(flops=6 * pairs * d0 * d1, bytes_accessed=6 << 20, transcendentals=rows * d0),
        name="backward",
    )(core, feat, sums, own, other, cot)


def keep_half(core, s, cot, wide, half):
    pairs, d0 = s.shape
    return pl.pallas_call(
        keep_kernel,
        out_shape=jax.ShapeDtypeStruct((d0, half), F32),
        in_specs=[SMEM] + [VMEM] * 3,
        out_specs=VMEM,
        compiler_params=pltpu.CompilerParams(vmem_limit_bytes=16 << 20),
        cost_estimate=pl.CostEstimate(flops=2 * pairs * d0 * half, bytes_accessed=4 << 20, transcendentals=0),
        name="keep_half",
    )(core, s, cot, wide)


def pool(s, w, bias):
    pairs, d0 = s.shape
    d1 = bias.shape[1]
    hbm = pl.BlockSpec(memory_space=pltpu.HBM)
    parts = 3
    return pl.pallas_call(
        pool_kernel,
        out_shape=jax.ShapeDtypeStruct((pairs, d1), BF16),
        in_specs=[VMEM] * 3,
        out_specs=hbm,
        scratch_shapes=[pltpu.VMEM((parts, pairs // parts, d1), BF16), pltpu.SemaphoreType.DMA((parts,))],
        compiler_params=pltpu.CompilerParams(vmem_limit_bytes=16 << 20),
        cost_estimate=pl.CostEstimate(flops=2 * pairs * d0 * d1, bytes_accessed=4 << 20, transcendentals=0),
        name="pool",
    )(s, w, bias)


def pack_kernel(core_ref, bases_hbm, embed_hbm, embed_bias_hbm, gain_hbm, proj_hbm, proj_bias_hbm,
                out_ref, inner_ref, outer_ref,
                bases_ref, embed_ref, embed_bias_ref, gain_ref, proj_ref, proj_bias_ref, rows_ref, block_ref, sems):
    kw, block, d1 = embed_ref.shape[0], proj_ref.shape[0], proj_ref.shape[1]
    copies, _, half = out_ref.shape
    taps, per = kw * 4, proj_bias_ref.shape[1]
    fetched = [
        pltpu.make_async_copy(source, target, sems.at[n])
        for n, (source, target) in enumerate((
            (bases_hbm, bases_ref), (embed_hbm, embed_ref), (embed_bias_hbm, embed_bias_ref),
            (gain_hbm, gain_ref), (proj_hbm, proj_ref), (proj_bias_hbm, proj_bias_ref)))
    ]
    for copy in fetched:
        copy.start()
    rows_ref[...] = jnp.zeros_like(rows_ref)
    for copy in fetched:
        copy.wait()
    first = bases_ref[:, :LANES] + 1
    last = bases_ref[:, bases_ref.shape[1] - LANES:] + 1
    even = core_ref[0] == 0
    inner_ref[...] = jnp.where(even, last, first)
    outer_ref[...] = jnp.where(even, first, last)
    for k in range(kw):
        rows_ref[4 * k:4 * k + 4, :block] = embed_ref[k].astype(F32)
    rows_ref[taps:taps + 1, :block] = embed_bias_ref[...].astype(F32)
    rows_ref[taps + 1:taps + 2, :block] = gain_ref[...].astype(F32)
    block_ref[...] = rows_ref[...].T[:block]
    block_ref[:1, 64:64 + per] = proj_bias_ref[...].astype(F32)
    edge = d1 - half

    @pl.when(even)
    def _():
        for i in range(copies):
            out_ref[i] = proj_ref[:, :half]

    @pl.when(jnp.logical_not(even))
    def _():
        for i in range(copies):
            out_ref[i, :, :edge] = proj_ref[:, half:]
            out_ref[i, :, edge:] = block_ref[...].astype(BF16)


def sum_kernel(scale, in_ref, out_ref):
    total = in_ref[0].astype(F32)
    for i in range(1, in_ref.shape[0]):
        total = total + in_ref[i].astype(F32)
    if scale != 1.0:
        total = total * scale
    total = total.astype(out_ref.dtype)
    for i in range(out_ref.shape[0]):
        out_ref[i] = total


def unpack_kernel(core_ref, total_ref, across_ref, embed_ref, embed_bias_ref, gain_ref, proj_ref, proj_bias_ref, rows_ref):
    kw, block, d1 = embed_ref.shape[0], proj_ref.shape[0], proj_ref.shape[1]
    half = total_ref.shape[1]
    taps, per, edge = kw * 4, proj_bias_ref.shape[1], d1 - half

    def place(left_ref, right_ref):
        proj_ref[:, :half] = left_ref[...]
        proj_ref[:, half:] = right_ref[:, :edge]
        rows_ref[:block, :] = right_ref[:, edge:]

    @pl.when(core_ref[0] == 0)
    def _():
        place(total_ref, across_ref)

    @pl.when(core_ref[0] != 0)
    def _():
        place(across_ref, total_ref)

    proj_bias_ref[...] = rows_ref[:1, 64:64 + per]
    rows_ref[block:, :] = jnp.zeros((LANES - block, LANES), F32)
    rows_ref[...] = rows_ref[...].T
    for k in range(kw):
        embed_ref[k] = rows_ref[4 * k:4 * k + 4, :block]
    embed_bias_ref[...] = rows_ref[taps:taps + 1, :block]
    gain_ref[...] = rows_ref[taps + 1:taps + 2, :block]


def local(bases, embed_weight, embed_bias, norm_gain, proj_weight, proj_bias, cotangent):
    kw = embed_weight.shape[0]
    shards, members = lax.axis_size("dp"), lax.axis_size("seq")
    block, d1 = proj_weight.shape
    per = proj_bias.shape[0]
    half = (d1 + LANES) // 2
    core = (lax.axis_index("seq") & 1).astype(jnp.int32).reshape(1)
    swap = [(i, i ^ 1) for i in range(members)]

    facing = [(i, i + 1 if i % 2 else i - 1) for i in range(1, members - 1)]

    hbm = pl.BlockSpec(memory_space=pltpu.HBM)
    gathered = (bases, embed_weight, embed_bias[None], norm_gain[None], proj_weight, proj_bias[None])
    piece, inner, outer = pl.pallas_call(
        pack_kernel,
        out_shape=(
            jax.ShapeDtypeStruct((shards, block, half), BF16),
            jax.ShapeDtypeStruct((1, LANES), jnp.int32),
            jax.ShapeDtypeStruct((1, LANES), jnp.int32),
        ),
        in_specs=[SMEM] + [hbm] * 6,
        out_specs=(VMEM,) * 3,
        scratch_shapes=[pltpu.VMEM(x.shape, x.dtype) for x in gathered] + [
            pltpu.VMEM((LANES, LANES), F32), pltpu.VMEM((block, LANES), F32), pltpu.SemaphoreType.DMA((6,))],
        compiler_params=pltpu.CompilerParams(vmem_limit_bytes=60 << 20),
        name="pack",
    )(core, *gathered)
    inner = lax.ppermute(inner, "seq", swap)
    outer = lax.ppermute(outer, "seq", facing)
    own = lax.all_to_all(piece, "dp", 0, 0, tiled=True).reshape(shards * block, half)
    feat, sums = make_features(core, inner, bases, outer, cotangent[0], kw, shards)
    own, feat, sums = lax.optimization_barrier((own, feat, sums))
    other = lax.ppermute(own, "seq", swap)

    cot = cotangent[0]
    theirs, s, wide, bias, w = backward(core, feat, sums, own, other, cot, kw, shards)
    came = lax.ppermute(theirs, "seq", swap)
    mine = keep_half(core, s, cot, wide, half)
    pooled = pool(s, w, bias)
    summed = (mine + came.astype(F32)).astype(BF16).reshape(shards, block, half)
    parts = lax.all_to_all(summed, "dp", 0, 0, tiled=True)

    def add_up(parts, scale, copies, kind):
        return pl.pallas_call(
            functools.partial(sum_kernel, scale),
            out_shape=jax.ShapeDtypeStruct((copies, block, half), kind),
            in_specs=[VMEM],
            out_specs=VMEM,
            compiler_params=pltpu.CompilerParams(vmem_limit_bytes=4 << 20),
            name="add_up",
        )(parts)

    groups = [[i for i in range(members) if i % 2 == c] for c in range(2)]
    spread = lax.all_to_all(add_up(parts, 1.0, members // 2, BF16), "seq", 0, 0, axis_index_groups=groups, tiled=True)
    total = add_up(spread, 0.125 / (cotangent.shape[1] * members * shards), 1, F32)[0]
    across = lax.ppermute(total, "seq", swap)
    grad_embed, grad_embed_bias, grad_gain, grad_proj, grad_proj_bias = pl.pallas_call(
        unpack_kernel,
        out_shape=(
            jax.ShapeDtypeStruct(embed_weight.shape, F32),
            jax.ShapeDtypeStruct((1, block), F32),
            jax.ShapeDtypeStruct((1, block), F32),
            jax.ShapeDtypeStruct((block, d1), F32),
            jax.ShapeDtypeStruct((1, per), F32),
        ),
        in_specs=[SMEM, VMEM, VMEM],
        out_specs=(VMEM,) * 5,
        scratch_shapes=[pltpu.VMEM((LANES, LANES), F32)],
        compiler_params=pltpu.CompilerParams(vmem_limit_bytes=4 << 20),
        name="unpack",
    )(core, total, across)
    return (pooled[None], grad_embed, grad_embed_bias[0], grad_gain[0], grad_proj, grad_proj_bias[0])


def solution(mesh):
    placed = (
        P("dp", "seq"),
        P(None, None, "dp"),
        P("dp"),
        P("dp"),
        P("dp", None),
        P("dp"),
        P("dp", "seq", None),
    )
    return jax.shard_map(
        local,
        mesh=mesh,
        in_specs=placed,
        out_specs=(
            P("dp", "seq", None),
            P(None, None, "dp"),
            P("dp"),
            P("dp"),
            P("dp", None),
            P("dp"),
        ),
        check_vma=False,
    )
```

```python
import functools

import jax
import jax.numpy as jnp
from jax import lax
from jax.experimental import pallas as pl
from jax.experimental.pallas import tpu as pltpu
from jax.sharding import PartitionSpec as P

F32, BF16 = jnp.float32, jnp.bfloat16
LANES = 128
GELU_A = 0.7978845608028654
GELU_B = 0.044715
GELU_K = (GELU_A * GELU_B) ** (1 / 3)
GELU_C = GELU_A / GELU_K
EPSILON = 1e-06


def dot(a, b, contract, precision=None):
    return lax.dot_general(a, b, ((contract[:1], contract[1:]), ((), ())), precision=precision, preferred_element_type=F32)


def iota(shape, dim):
    return lax.broadcasted_iota(jnp.int32, shape, dim)


def by_owner(shards, d1):
    per = d1 // shards
    column = iota((LANES, d1), 1)
    owner = (column * 2341) >> 16
    spread = (iota((LANES, d1), 0) == column - owner * per + 64).astype(F32)
    return owner[:shards] == iota((shards, d1), 0), spread


def feature_kernel(kw, tile, core_ref, inner_ref, bases_ref, outer_ref, cot_ref, feat_ref, sums_ref, code_ref, perm_ref):
    rows = bases_ref.shape[1]
    pair_tile, reach, taps = tile // 2, kw // 2, kw * 4

    @pl.when(core_ref[0] == 0)
    def _():
        code_ref[:, :LANES] = outer_ref[...].astype(F32)
        code_ref[:, LANES + rows:] = inner_ref[...].astype(F32)

    @pl.when(core_ref[0] != 0)
    def _():
        code_ref[:, :LANES] = inner_ref[...].astype(F32)
        code_ref[:, LANES + rows:] = outer_ref[...].astype(F32)

    code_ref[:, LANES:LANES + rows] = (bases_ref[...] + 1).astype(F32)
    source, place = iota((tile, tile), 0), iota((tile, tile), 1)
    perm_ref[...] = (source == jnp.where(place < pair_tile, 2 * place, 2 * (place - pair_tile) + 1)).astype(BF16)
    repeat = ((iota((LANES, 16), 0) >> 2) == iota((LANES, 16), 1)).astype(BF16)
    letter = (iota((LANES, tile), 0) & 3) + 1
    line = iota((LANES, tile), 0)
    for t in range(rows // tile):
        window = code_ref[:, t * tile:t * tile + tile + 2 * LANES]
        start = LANES - reach
        shifted = jnp.concatenate([window[:, start + k:start + k + tile] for k in range(kw)] + [jnp.zeros((1, tile), F32)], axis=0)
        spreaded = dot(repeat, shifted.astype(BF16), (1, 0))
        hot = ((spreaded == letter.astype(F32)) & (line < taps)) | (line == taps)
        ordered = dot(hot.astype(F32).astype(BF16), perm_ref[...], (1, 0))
        feat_ref[:, t * tile:(t + 1) * tile] = ordered.astype(BF16)

    shards = sums_ref.shape[0]
    owned, spread = by_owner(shards, cot_ref.shape[1])
    sums = 4.0 * jnp.sum(cot_ref[...].astype(F32), axis=0, keepdims=True)
    sums_ref[...] = dot(jnp.where(owned, sums, 0.0), spread, (1, 1), lax.Precision.HIGHEST)


def step_kernel(dims, core_ref, feat_ref, sums_ref, own_ref, other_ref, cot_ref,
                theirs_ref, s_ref, wide_ref, bias_ref, w_ref,
                we_ref, emb_ref, ga_ref, ge_ref, gew_ref):
    kw, shards, d0, d1, rows, tile, chunk = dims
    half = w_ref.shape[1] // 2
    pair_tile = tile // 2
    taps = kw * 4
    core = core_ref[0]
    block = d0 // shards

    @pl.when(core == 0)
    def _():
        w_ref[:, :half] = own_ref[...]
        w_ref[:, half:] = other_ref[...]

    @pl.when(core != 0)
    def _():
        w_ref[:, :half] = other_ref[...]
        w_ref[:, half:] = own_ref[...]

    wide = w_ref[:, d1:].astype(F32)
    wide_ref[...] = wide
    we_ref[...] = wide.T.astype(BF16)
    gain = we_ref[pl.ds(64 - 8, 8), :].astype(F32)[5:6, :]
    gain_y = gain * GELU_K

    owned, spread = by_owner(shards, d1)
    pieces = wide_ref[pl.ds(0, shards, stride=block), :]
    bias_ref[...] = jnp.sum(jnp.where(owned, dot(pieces.astype(BF16), spread.astype(BF16), (1, 0)), 0.0), axis=0, keepdims=True)

    for t in range(rows // tile):
        at = t * tile
        emb_ref[at:at + tile, :] = dot(feat_ref[:, at:at + tile], we_ref[...], (0, 0)).astype(BF16)
        half_at = t * pair_tile
        ga_ref[half_at:half_at + pair_tile, :] = dot(cot_ref[half_at:half_at + pair_tile, :], w_ref[:, :d1], (1, 1))

        def side(start, grad):
            values = emb_ref[pl.ds(start, chunk), :].astype(F32)
            inverse = lax.rsqrt(jnp.sum(values * values, axis=1, keepdims=True) * (1.0 / d0) + EPSILON)
            y = (values * inverse) * gain_y
            square = y * y
            tanh = jnp.tanh(y * (GELU_C + square))
            above, below = 1.0 + tanh, 1.0 - tanh
            activated = y * above
            slope = above + (activated * below) * (GELU_C + 3.0 * square)
            grad_normed = grad * slope
            toward_gain = grad_normed * y
            shared = jnp.sum(toward_gain, axis=1, keepdims=True) * (inverse * inverse * (1.0 / (GELU_K * d0)))
            ge_ref[pl.ds(start, chunk), :] = (inverse * (grad_normed * gain) - values * shared).astype(BF16)
            return activated, toward_gain

        def body(i, total):
            first = pl.multiple_of(at + i * chunk, chunk)
            second = pl.multiple_of(at + pair_tile + i * chunk, chunk)
            pair_at = pl.multiple_of(half_at + i * chunk, chunk)
            grad = ga_ref[pl.ds(pair_at, chunk), :]
            act_even, gain_even = side(first, grad)
            act_odd, gain_odd = side(second, grad)
            s_ref[pl.ds(pair_at, chunk), :] = (act_even + act_odd).astype(BF16)
            both = gain_even + gain_odd
            for r in range(0, chunk, 8):
                total = total + both[r:r + 8]
            return total

        start_total = jnp.zeros((8, d0), F32)
        gain_total = lax.fori_loop(0, pair_tile // chunk, body, start_total, unroll=True)
        part = dot(feat_ref[:, at:at + tile], ge_ref[at:at + tile, :], (1, 0))
        is_gain = iota((LANES, d0), 0) == taps + 1
        part = jnp.where(is_gain, jnp.sum(gain_total, axis=0, keepdims=True) / gain_y, part)
        if t == 0:
            gew_ref[...] = part
        else:
            gew_ref[...] += part

    wide_ref[...] = gew_ref[...].T
    wide_ref[pl.ds(0, shards, stride=block), :] = wide_ref[pl.ds(0, shards, stride=block), :] + sums_ref[...]

    @pl.when(core == 0)
    def _():
        right_half(s_ref, cot_ref, wide_ref, theirs_ref)

    @pl.when(core != 0)
    def _():
        left_half(s_ref, cot_ref, theirs_ref)


def left_half(s_ref, cot_ref, out_ref):
    half = out_ref.shape[1]
    out_ref[...] = (dot(s_ref[...], cot_ref[:, :half], (0, 0)) * (1.0 / GELU_K)).astype(out_ref.dtype)


def right_half(s_ref, cot_ref, wide_ref, out_ref):
    half = out_ref.shape[1]
    edge = cot_ref.shape[1] - half
    out_ref[:, :edge] = (dot(s_ref[...], cot_ref[:, half:], (0, 0)) * (1.0 / GELU_K)).astype(out_ref.dtype)
    out_ref[:, edge:] = wide_ref[...].astype(out_ref.dtype)


def keep_kernel(core_ref, s_ref, cot_ref, wide_ref, mine_ref):
    @pl.when(core_ref[0] == 0)
    def _():
        left_half(s_ref, cot_ref, mine_ref)

    @pl.when(core_ref[0] != 0)
    def _():
        right_half(s_ref, cot_ref, wide_ref, mine_ref)


def pool_kernel(s_ref, w_ref, bias_ref, pooled_hbm, stage_ref, sems):
    parts, step, d1 = stage_ref.shape
    copies = [pltpu.make_async_copy(stage_ref.at[n], pooled_hbm.at[pl.ds(n * step, step), :], sems.at[n]) for n in range(parts)]
    for n in range(parts):
        mixed = dot(s_ref[n * step:(n + 1) * step, :], w_ref[:, :d1], (1, 0))
        stage_ref[n] = ((0.25 / GELU_K) * mixed + bias_ref[...]).astype(BF16)
        copies[n].start()
    for copy in copies:
        copy.wait()


VMEM = pl.BlockSpec(memory_space=pltpu.VMEM)
SMEM = pl.BlockSpec(memory_space=pltpu.SMEM)
TILE, CHUNK = 1536, 32


def make_features(core, inner, bases, outer, cot, kw, shards):
    rows = bases.shape[1]
    return pl.pallas_call(
        functools.partial(feature_kernel, kw, TILE),
        out_shape=(jax.ShapeDtypeStruct((LANES, rows), BF16), jax.ShapeDtypeStruct((shards, LANES), F32)),
        in_specs=[SMEM] + [VMEM] * 4,
        out_specs=(VMEM, VMEM),
        scratch_shapes=[pltpu.VMEM((1, rows + 2 * LANES), F32), pltpu.VMEM((TILE, TILE), BF16)],
        compiler_params=pltpu.CompilerParams(vmem_limit_bytes=16 << 20),
        cost_estimate=pl.CostEstimate(flops=2 * LANES * TILE * rows, bytes_accessed=2 << 20, transcendentals=0),
        name="features",
    )(core, inner, bases, outer, cot)


def backward(core, feat, sums, own, other, cot, kw, shards):
    d0, half = own.shape
    pairs, d1 = cot.shape
    rows = 2 * pairs
    dims = (kw, shards, d0, d1, rows, TILE, CHUNK)
    return pl.pallas_call(
        functools.partial(step_kernel, dims),
        out_shape=(
            jax.ShapeDtypeStruct((d0, half), BF16),
            jax.ShapeDtypeStruct((pairs, d0), BF16),
            jax.ShapeDtypeStruct((d0, LANES), F32),
            jax.ShapeDtypeStruct((1, d1), F32),
            jax.ShapeDtypeStruct((d0, 2 * half), BF16),
        ),
        in_specs=[SMEM] + [VMEM] * 5,
        out_specs=(VMEM,) * 5,
        scratch_shapes=[
            pltpu.VMEM((LANES, d0), BF16),
            pltpu.VMEM((rows, d0), BF16),
            pltpu.VMEM((pairs, d0), F32),
            pltpu.VMEM((rows, d0), BF16),
            pltpu.VMEM((LANES, d0), F32),
        ],
        compiler_params=pltpu.CompilerParams(vmem_limit_bytes=28 << 20),
        cost_estimate=pl.CostEstimate(flops=6 * pairs * d0 * d1, bytes_accessed=6 << 20, transcendentals=rows * d0),
        name="backward",
    )(core, feat, sums, own, other, cot)


def keep_half(core, s, cot, wide, half):
    pairs, d0 = s.shape
    return pl.pallas_call(
        keep_kernel,
        out_shape=jax.ShapeDtypeStruct((d0, half), F32),
        in_specs=[SMEM] + [VMEM] * 3,
        out_specs=VMEM,
        compiler_params=pltpu.CompilerParams(vmem_limit_bytes=16 << 20),
        cost_estimate=pl.CostEstimate(flops=2 * pairs * d0 * half, bytes_accessed=4 << 20, transcendentals=0),
        name="keep_half",
    )(core, s, cot, wide)


def pool(s, w, bias):
    pairs, d0 = s.shape
    d1 = bias.shape[1]
    hbm = pl.BlockSpec(memory_space=pltpu.HBM)
    parts = 3
    return pl.pallas_call(
        pool_kernel,
        out_shape=jax.ShapeDtypeStruct((pairs, d1), BF16),
        in_specs=[VMEM] * 3,
        out_specs=hbm,
        scratch_shapes=[pltpu.VMEM((parts, pairs // parts, d1), BF16), pltpu.SemaphoreType.DMA((parts,))],
        compiler_params=pltpu.CompilerParams(vmem_limit_bytes=16 << 20),
        cost_estimate=pl.CostEstimate(flops=2 * pairs * d0 * d1, bytes_accessed=4 << 20, transcendentals=0),
        name="pool",
    )(s, w, bias)


def pack_kernel(core_ref, bases_hbm, embed_hbm, embed_bias_hbm, gain_hbm, proj_hbm, proj_bias_hbm,
                out_ref, inner_ref, outer_ref,
                bases_ref, embed_ref, embed_bias_ref, gain_ref, proj_ref, proj_bias_ref, rows_ref, block_ref, sems):
    kw, block, d1 = embed_ref.shape[0], proj_ref.shape[0], proj_ref.shape[1]
    copies, _, half = out_ref.shape
    taps, per = kw * 4, proj_bias_ref.shape[1]
    fetched = [
        pltpu.make_async_copy(source, target, sems.at[n])
        for n, (source, target) in enumerate((
            (bases_hbm, bases_ref), (embed_hbm, embed_ref), (embed_bias_hbm, embed_bias_ref),
            (gain_hbm, gain_ref), (proj_hbm, proj_ref), (proj_bias_hbm, proj_bias_ref)))
    ]
    for copy in fetched:
        copy.start()
    rows_ref[...] = jnp.zeros_like(rows_ref)
    for copy in fetched:
        copy.wait()
    first = bases_ref[:, :LANES] + 1
    last = bases_ref[:, bases_ref.shape[1] - LANES:] + 1
    even = core_ref[0] == 0
    inner_ref[...] = jnp.where(even, last, first)
    outer_ref[...] = jnp.where(even, first, last)
    for k in range(kw):
        rows_ref[4 * k:4 * k + 4, :block] = embed_ref[k].astype(F32)
    rows_ref[taps:taps + 1, :block] = embed_bias_ref[...].astype(F32)
    rows_ref[taps + 1:taps + 2, :block] = gain_ref[...].astype(F32)
    block_ref[...] = rows_ref[...].T[:block]
    block_ref[:1, 64:64 + per] = proj_bias_ref[...].astype(F32)
    edge = d1 - half

    @pl.when(even)
    def _():
        for i in range(copies):
            out_ref[i] = proj_ref[:, :half]

    @pl.when(jnp.logical_not(even))
    def _():
        for i in range(copies):
            out_ref[i, :, :edge] = proj_ref[:, half:]
            out_ref[i, :, edge:] = block_ref[...].astype(BF16)


def sum_kernel(scale, in_ref, out_ref):
    total = in_ref[0].astype(F32)
    for i in range(1, in_ref.shape[0]):
        total = total + in_ref[i].astype(F32)
    if scale != 1.0:
        total = total * scale
    total = total.astype(out_ref.dtype)
    for i in range(out_ref.shape[0]):
        out_ref[i] = total


def unpack_kernel(scale, parts_ref, embed_ref, embed_bias_ref, gain_ref, proj_ref, proj_bias_ref, rows_ref):
    kw, block, d1 = embed_ref.shape[0], proj_ref.shape[0], proj_ref.shape[1]
    half = parts_ref.shape[2]
    taps, per, edge = kw * 4, proj_bias_ref.shape[1], d1 - half
    right = (parts_ref[1] + parts_ref[3]) * scale
    proj_ref[:, :half] = (parts_ref[0] + parts_ref[2]) * scale
    proj_ref[:, half:] = right[:, :edge]
    rows_ref[:block, :] = right[:, edge:]
    proj_bias_ref[...] = rows_ref[:1, 64:64 + per]
    rows_ref[block:, :] = jnp.zeros((LANES - block, LANES), F32)
    rows_ref[...] = rows_ref[...].T
    for k in range(kw):
        embed_ref[k] = rows_ref[4 * k:4 * k + 4, :block]
    embed_bias_ref[...] = rows_ref[taps:taps + 1, :block]
    gain_ref[...] = rows_ref[taps + 1:taps + 2, :block]


def local(bases, embed_weight, embed_bias, norm_gain, proj_weight, proj_bias, cotangent):
    kw = embed_weight.shape[0]
    shards, members = lax.axis_size("dp"), lax.axis_size("seq")
    block, d1 = proj_weight.shape
    per = proj_bias.shape[0]
    half = (d1 + LANES) // 2
    core = (lax.axis_index("seq") & 1).astype(jnp.int32).reshape(1)
    swap = [(i, i ^ 1) for i in range(members)]

    facing = [(i, i + 1 if i % 2 else i - 1) for i in range(1, members - 1)]

    hbm = pl.BlockSpec(memory_space=pltpu.HBM)
    gathered = (bases, embed_weight, embed_bias[None], norm_gain[None], proj_weight, proj_bias[None])
    piece, inner, outer = pl.pallas_call(
        pack_kernel,
        out_shape=(
            jax.ShapeDtypeStruct((shards, block, half), BF16),
            jax.ShapeDtypeStruct((1, LANES), jnp.int32),
            jax.ShapeDtypeStruct((1, LANES), jnp.int32),
        ),
        in_specs=[SMEM] + [hbm] * 6,
        out_specs=(VMEM,) * 3,
        scratch_shapes=[pltpu.VMEM(x.shape, x.dtype) for x in gathered] + [
            pltpu.VMEM((LANES, LANES), F32), pltpu.VMEM((block, LANES), F32), pltpu.SemaphoreType.DMA((6,))],
        compiler_params=pltpu.CompilerParams(vmem_limit_bytes=60 << 20),
        name="pack",
    )(core, *gathered)
    inner = lax.ppermute(inner, "seq", swap)
    outer = lax.ppermute(outer, "seq", facing)
    own = lax.all_to_all(piece, "dp", 0, 0, tiled=True).reshape(shards * block, half)
    feat, sums = make_features(core, inner, bases, outer, cotangent[0], kw, shards)
    own, feat, sums = lax.optimization_barrier((own, feat, sums))
    other = lax.ppermute(own, "seq", swap)

    cot = cotangent[0]
    theirs, s, wide, bias, w = backward(core, feat, sums, own, other, cot, kw, shards)
    came = lax.ppermute(theirs, "seq", swap)
    mine = keep_half(core, s, cot, wide, half)
    pooled = pool(s, w, bias)
    summed = (mine + came.astype(F32)).astype(BF16).reshape(shards, block, half)
    parts = lax.all_to_all(summed, "dp", 0, 0, tiled=True)

    def add_up(parts, scale, copies, kind):
        return pl.pallas_call(
            functools.partial(sum_kernel, scale),
            out_shape=jax.ShapeDtypeStruct((copies, block, half), kind),
            in_specs=[VMEM],
            out_specs=VMEM,
            compiler_params=pltpu.CompilerParams(vmem_limit_bytes=4 << 20),
            name="add_up",
        )(parts)

    along_x = [list(range(i, members, 4)) for i in range(4)]
    within = [list(range(i, i + 4)) for i in range(0, members, 4)]
    spread = lax.all_to_all(add_up(parts, 1.0, members // 4, BF16), "seq", 0, 0, axis_index_groups=along_x, tiled=True)
    spread = lax.all_to_all(add_up(spread, 1.0, 4, F32), "seq", 0, 0, axis_index_groups=within, tiled=True)
    scale = 0.125 / (cotangent.shape[1] * members * shards)
    grad_embed, grad_embed_bias, grad_gain, grad_proj, grad_proj_bias = pl.pallas_call(
        functools.partial(unpack_kernel, scale),
        out_shape=(
            jax.ShapeDtypeStruct(embed_weight.shape, F32),
            jax.ShapeDtypeStruct((1, block), F32),
            jax.ShapeDtypeStruct((1, block), F32),
            jax.ShapeDtypeStruct((block, d1), F32),
            jax.ShapeDtypeStruct((1, per), F32),
        ),
        in_specs=[VMEM],
        out_specs=(VMEM,) * 5,
        scratch_shapes=[pltpu.VMEM((LANES, LANES), F32)],
        compiler_params=pltpu.CompilerParams(vmem_limit_bytes=4 << 20),
        name="unpack",
    )(spread)
    return (pooled[None], grad_embed, grad_embed_bias[0], grad_gain[0], grad_proj, grad_proj_bias[0])


def solution(mesh):
    placed = (
        P("dp", "seq"),
        P(None, None, "dp"),
        P("dp"),
        P("dp"),
        P("dp", None),
        P("dp"),
        P("dp", "seq", None),
    )
    return jax.shard_map(
        local,
        mesh=mesh,
        in_specs=placed,
        out_specs=(
            P("dp", "seq", None),
            P(None, None, "dp"),
            P("dp"),
            P("dp"),
            P("dp", None),
            P("dp"),
        ),
        check_vma=False,
    )
```

```python
import functools

import jax
import jax.numpy as jnp
from jax import lax
from jax.experimental import pallas as pl
from jax.experimental.pallas import tpu as pltpu
from jax.sharding import PartitionSpec as P

F32, BF16 = jnp.float32, jnp.bfloat16
LANES = 128
GELU_A = 0.7978845608028654
GELU_B = 0.044715
GELU_K = (GELU_A * GELU_B) ** (1 / 3)
GELU_C = GELU_A / GELU_K
EPSILON = 1e-06


def dot(a, b, contract, precision=None):
    return lax.dot_general(a, b, ((contract[:1], contract[1:]), ((), ())), precision=precision, preferred_element_type=F32)


def iota(shape, dim):
    return lax.broadcasted_iota(jnp.int32, shape, dim)


def by_owner(shards, d1):
    per = d1 // shards
    column = iota((LANES, d1), 1)
    owner = (column * 2341) >> 16
    spread = (iota((LANES, d1), 0) == column - owner * per + 64).astype(F32)
    return owner[:shards] == iota((shards, d1), 0), spread


def feature_kernel(kw, tile, core_ref, inner_ref, bases_ref, outer_ref, cot_ref, feat_ref, sums_ref, code_ref, perm_ref):
    rows = bases_ref.shape[1]
    pair_tile, reach, taps = tile // 2, kw // 2, kw * 4

    @pl.when(core_ref[0] == 0)
    def _():
        code_ref[:, :LANES] = outer_ref[...].astype(F32)
        code_ref[:, LANES + rows:] = inner_ref[...].astype(F32)

    @pl.when(core_ref[0] != 0)
    def _():
        code_ref[:, :LANES] = inner_ref[...].astype(F32)
        code_ref[:, LANES + rows:] = outer_ref[...].astype(F32)

    code_ref[:, LANES:LANES + rows] = (bases_ref[...] + 1).astype(F32)
    source, place = iota((tile, tile), 0), iota((tile, tile), 1)
    perm_ref[...] = (source == jnp.where(place < pair_tile, 2 * place, 2 * (place - pair_tile) + 1)).astype(BF16)
    repeat = ((iota((LANES, 16), 0) >> 2) == iota((LANES, 16), 1)).astype(BF16)
    letter = (iota((LANES, tile), 0) & 3) + 1
    line = iota((LANES, tile), 0)
    for t in range(rows // tile):
        window = code_ref[:, t * tile:t * tile + tile + 2 * LANES]
        start = LANES - reach
        shifted = jnp.concatenate([window[:, start + k:start + k + tile] for k in range(kw)] + [jnp.zeros((1, tile), F32)], axis=0)
        spreaded = dot(repeat, shifted.astype(BF16), (1, 0))
        hot = ((spreaded == letter.astype(F32)) & (line < taps)) | (line == taps)
        ordered = dot(hot.astype(F32).astype(BF16), perm_ref[...], (1, 0))
        feat_ref[:, t * tile:(t + 1) * tile] = ordered.astype(BF16)

    shards = sums_ref.shape[0]
    owned, spread = by_owner(shards, cot_ref.shape[1])
    sums = 4.0 * jnp.sum(cot_ref[...].astype(F32), axis=0, keepdims=True)
    sums_ref[...] = dot(jnp.where(owned, sums, 0.0), spread, (1, 1), lax.Precision.HIGHEST)


def step_kernel(dims, core_ref, feat_ref, sums_ref, own_ref, other_ref, cot_ref,
                theirs_ref, s_ref, wide_ref, bias_ref, w_ref,
                we_ref, emb_ref, ga_ref, ge_ref, gew_ref):
    kw, shards, d0, d1, rows, tile, chunk = dims
    half = w_ref.shape[1] // 2
    pair_tile = tile // 2
    taps = kw * 4
    core = core_ref[0]
    block = d0 // shards

    @pl.when(core == 0)
    def _():
        w_ref[:, :half] = own_ref[...]
        w_ref[:, half:] = other_ref[...]

    @pl.when(core != 0)
    def _():
        w_ref[:, :half] = other_ref[...]
        w_ref[:, half:] = own_ref[...]

    wide = w_ref[:, d1:].astype(F32)
    wide_ref[...] = wide
    we_ref[...] = wide.T.astype(BF16)
    gain = we_ref[pl.ds(64 - 8, 8), :].astype(F32)[5:6, :]
    gain_y = gain * GELU_K

    owned, spread = by_owner(shards, d1)
    pieces = wide_ref[pl.ds(0, shards, stride=block), :]
    bias_ref[...] = jnp.sum(jnp.where(owned, dot(pieces.astype(BF16), spread.astype(BF16), (1, 0)), 0.0), axis=0, keepdims=True)

    for t in range(rows // tile):
        at = t * tile
        emb_ref[at:at + tile, :] = dot(feat_ref[:, at:at + tile], we_ref[...], (0, 0)).astype(BF16)
        half_at = t * pair_tile
        ga_ref[half_at:half_at + pair_tile, :] = dot(cot_ref[half_at:half_at + pair_tile, :], w_ref[:, :d1], (1, 1))

        def side(start, grad):
            values = emb_ref[pl.ds(start, chunk), :].astype(F32)
            inverse = lax.rsqrt(jnp.sum(values * values, axis=1, keepdims=True) * (1.0 / d0) + EPSILON)
            y = (values * inverse) * gain_y
            square = y * y
            tanh = jnp.tanh(y * (GELU_C + square))
            above, below = 1.0 + tanh, 1.0 - tanh
            activated = y * above
            slope = above + (activated * below) * (GELU_C + 3.0 * square)
            grad_normed = grad * slope
            toward_gain = grad_normed * y
            shared = jnp.sum(toward_gain, axis=1, keepdims=True) * (inverse * inverse * (1.0 / (GELU_K * d0)))
            ge_ref[pl.ds(start, chunk), :] = (inverse * (grad_normed * gain) - values * shared).astype(BF16)
            return activated, toward_gain

        def body(i, total):
            first = pl.multiple_of(at + i * chunk, chunk)
            second = pl.multiple_of(at + pair_tile + i * chunk, chunk)
            pair_at = pl.multiple_of(half_at + i * chunk, chunk)
            grad = ga_ref[pl.ds(pair_at, chunk), :]
            act_even, gain_even = side(first, grad)
            act_odd, gain_odd = side(second, grad)
            s_ref[pl.ds(pair_at, chunk), :] = (act_even + act_odd).astype(BF16)
            both = gain_even + gain_odd
            for r in range(0, chunk, 8):
                total = total + both[r:r + 8]
            return total

        start_total = jnp.zeros((8, d0), F32)
        gain_total = lax.fori_loop(0, pair_tile // chunk, body, start_total, unroll=True)
        part = dot(feat_ref[:, at:at + tile], ge_ref[at:at + tile, :], (1, 0))
        is_gain = iota((LANES, d0), 0) == taps + 1
        part = jnp.where(is_gain, jnp.sum(gain_total, axis=0, keepdims=True) / gain_y, part)
        if t == 0:
            gew_ref[...] = part
        else:
            gew_ref[...] += part

    wide_ref[...] = gew_ref[...].T
    wide_ref[pl.ds(0, shards, stride=block), :] = wide_ref[pl.ds(0, shards, stride=block), :] + sums_ref[...]

    @pl.when(core == 0)
    def _():
        right_half(s_ref, cot_ref, wide_ref, theirs_ref)

    @pl.when(core != 0)
    def _():
        left_half(s_ref, cot_ref, theirs_ref)


def left_half(s_ref, cot_ref, out_ref):
    half = out_ref.shape[1]
    out_ref[...] = (dot(s_ref[...], cot_ref[:, :half], (0, 0)) * (1.0 / GELU_K)).astype(out_ref.dtype)


def right_half(s_ref, cot_ref, wide_ref, out_ref):
    half = out_ref.shape[1]
    edge = cot_ref.shape[1] - half
    out_ref[:, :edge] = (dot(s_ref[...], cot_ref[:, half:], (0, 0)) * (1.0 / GELU_K)).astype(out_ref.dtype)
    out_ref[:, edge:] = wide_ref[...].astype(out_ref.dtype)


def keep_kernel(core_ref, s_ref, cot_ref, wide_ref, mine_ref):
    @pl.when(core_ref[0] == 0)
    def _():
        left_half(s_ref, cot_ref, mine_ref)

    @pl.when(core_ref[0] != 0)
    def _():
        right_half(s_ref, cot_ref, wide_ref, mine_ref)


def pool_kernel(s_ref, w_ref, bias_ref, pooled_hbm, stage_ref, sems):
    parts, step, d1 = stage_ref.shape
    copies = [pltpu.make_async_copy(stage_ref.at[n], pooled_hbm.at[pl.ds(n * step, step), :], sems.at[n]) for n in range(parts)]
    for n in range(parts):
        mixed = dot(s_ref[n * step:(n + 1) * step, :], w_ref[:, :d1], (1, 0))
        stage_ref[n] = ((0.25 / GELU_K) * mixed + bias_ref[...]).astype(BF16)
        copies[n].start()
    for copy in copies:
        copy.wait()


VMEM = pl.BlockSpec(memory_space=pltpu.VMEM)
SMEM = pl.BlockSpec(memory_space=pltpu.SMEM)
TILE, CHUNK = 1536, 32


def make_features(core, inner, bases, outer, cot, kw, shards):
    rows = bases.shape[1]
    return pl.pallas_call(
        functools.partial(feature_kernel, kw, TILE),
        out_shape=(jax.ShapeDtypeStruct((LANES, rows), BF16), jax.ShapeDtypeStruct((shards, LANES), F32)),
        in_specs=[SMEM] + [VMEM] * 4,
        out_specs=(VMEM, VMEM),
        scratch_shapes=[pltpu.VMEM((1, rows + 2 * LANES), F32), pltpu.VMEM((TILE, TILE), BF16)],
        compiler_params=pltpu.CompilerParams(vmem_limit_bytes=16 << 20),
        cost_estimate=pl.CostEstimate(flops=2 * LANES * TILE * rows, bytes_accessed=2 << 20, transcendentals=0),
        name="features",
    )(core, inner, bases, outer, cot)


def backward(core, feat, sums, own, other, cot, kw, shards):
    d0, half = own.shape
    pairs, d1 = cot.shape
    rows = 2 * pairs
    dims = (kw, shards, d0, d1, rows, TILE, CHUNK)
    return pl.pallas_call(
        functools.partial(step_kernel, dims),
        out_shape=(
            jax.ShapeDtypeStruct((d0, half), BF16),
            jax.ShapeDtypeStruct((pairs, d0), BF16),
            jax.ShapeDtypeStruct((d0, LANES), F32),
            jax.ShapeDtypeStruct((1, d1), F32),
            jax.ShapeDtypeStruct((d0, 2 * half), BF16),
        ),
        in_specs=[SMEM] + [VMEM] * 5,
        out_specs=(VMEM,) * 5,
        scratch_shapes=[
            pltpu.VMEM((LANES, d0), BF16),
            pltpu.VMEM((rows, d0), BF16),
            pltpu.VMEM((pairs, d0), F32),
            pltpu.VMEM((rows, d0), BF16),
            pltpu.VMEM((LANES, d0), F32),
        ],
        compiler_params=pltpu.CompilerParams(vmem_limit_bytes=28 << 20),
        cost_estimate=pl.CostEstimate(flops=6 * pairs * d0 * d1, bytes_accessed=6 << 20, transcendentals=rows * d0),
        name="backward",
    )(core, feat, sums, own, other, cot)


def keep_half(core, s, cot, wide, half):
    pairs, d0 = s.shape
    return pl.pallas_call(
        keep_kernel,
        out_shape=jax.ShapeDtypeStruct((d0, half), F32),
        in_specs=[SMEM] + [VMEM] * 3,
        out_specs=VMEM,
        compiler_params=pltpu.CompilerParams(vmem_limit_bytes=16 << 20),
        cost_estimate=pl.CostEstimate(flops=2 * pairs * d0 * half, bytes_accessed=4 << 20, transcendentals=0),
        name="keep_half",
    )(core, s, cot, wide)


def pool(s, w, bias):
    pairs, d0 = s.shape
    d1 = bias.shape[1]
    hbm = pl.BlockSpec(memory_space=pltpu.HBM)
    parts = 3
    return pl.pallas_call(
        pool_kernel,
        out_shape=jax.ShapeDtypeStruct((pairs, d1), BF16),
        in_specs=[VMEM] * 3,
        out_specs=hbm,
        scratch_shapes=[pltpu.VMEM((parts, pairs // parts, d1), BF16), pltpu.SemaphoreType.DMA((parts,))],
        compiler_params=pltpu.CompilerParams(vmem_limit_bytes=16 << 20),
        cost_estimate=pl.CostEstimate(flops=2 * pairs * d0 * d1, bytes_accessed=4 << 20, transcendentals=0),
        name="pool",
    )(s, w, bias)


def pack_kernel(core_ref, bases_hbm, embed_hbm, embed_bias_hbm, gain_hbm, proj_hbm, proj_bias_hbm,
                out_ref, inner_ref, outer_ref,
                bases_ref, embed_ref, embed_bias_ref, gain_ref, proj_ref, proj_bias_ref, rows_ref, block_ref, sems):
    kw, block, d1 = embed_ref.shape[0], proj_ref.shape[0], proj_ref.shape[1]
    copies, _, half = out_ref.shape
    taps, per = kw * 4, proj_bias_ref.shape[1]
    fetched = [
        pltpu.make_async_copy(source, target, sems.at[n])
        for n, (source, target) in enumerate((
            (bases_hbm, bases_ref), (embed_hbm, embed_ref), (embed_bias_hbm, embed_bias_ref),
            (gain_hbm, gain_ref), (proj_hbm, proj_ref), (proj_bias_hbm, proj_bias_ref)))
    ]
    for copy in fetched:
        copy.start()
    rows_ref[...] = jnp.zeros_like(rows_ref)
    for copy in fetched:
        copy.wait()
    first = bases_ref[:, :LANES] + 1
    last = bases_ref[:, bases_ref.shape[1] - LANES:] + 1
    even = core_ref[0] == 0
    inner_ref[...] = jnp.where(even, last, first)
    outer_ref[...] = jnp.where(even, first, last)
    for k in range(kw):
        rows_ref[4 * k:4 * k + 4, :block] = embed_ref[k].astype(F32)
    rows_ref[taps:taps + 1, :block] = embed_bias_ref[...].astype(F32)
    rows_ref[taps + 1:taps + 2, :block] = gain_ref[...].astype(F32)
    block_ref[...] = rows_ref[...].T[:block]
    block_ref[:1, 64:64 + per] = proj_bias_ref[...].astype(F32)
    edge = d1 - half

    @pl.when(even)
    def _():
        for i in range(copies):
            out_ref[i] = proj_ref[:, :half]

    @pl.when(jnp.logical_not(even))
    def _():
        for i in range(copies):
            out_ref[i, :, :edge] = proj_ref[:, half:]
            out_ref[i, :, edge:] = block_ref[...].astype(BF16)


def sum_kernel(scale, in_ref, out_ref):
    total = in_ref[0].astype(F32)
    for i in range(1, in_ref.shape[0]):
        total = total + in_ref[i].astype(F32)
    if scale != 1.0:
        total = total * scale
    total = total.astype(out_ref.dtype)
    for i in range(out_ref.shape[0]):
        out_ref[i] = total


def unpack_kernel(core_ref, total_ref, across_ref, embed_ref, embed_bias_ref, gain_ref, proj_ref, proj_bias_ref, rows_ref):
    kw, block, d1 = embed_ref.shape[0], proj_ref.shape[0], proj_ref.shape[1]
    half = total_ref.shape[1]
    taps, per, edge = kw * 4, proj_bias_ref.shape[1], d1 - half

    def place(left_ref, right_ref):
        proj_ref[:, :half] = left_ref[...]
        proj_ref[:, half:] = right_ref[:, :edge]
        rows_ref[:block, :] = right_ref[:, edge:]

    @pl.when(core_ref[0] == 0)
    def _():
        place(total_ref, across_ref)

    @pl.when(core_ref[0] != 0)
    def _():
        place(across_ref, total_ref)

    proj_bias_ref[...] = rows_ref[:1, 64:64 + per]
    rows_ref[block:, :] = jnp.zeros((LANES - block, LANES), F32)
    rows_ref[...] = rows_ref[...].T
    for k in range(kw):
        embed_ref[k] = rows_ref[4 * k:4 * k + 4, :block]
    embed_bias_ref[...] = rows_ref[taps:taps + 1, :block]
    gain_ref[...] = rows_ref[taps + 1:taps + 2, :block]


def local(bases, embed_weight, embed_bias, norm_gain, proj_weight, proj_bias, cotangent):
    kw = embed_weight.shape[0]
    shards, members = lax.axis_size("dp"), lax.axis_size("seq")
    block, d1 = proj_weight.shape
    per = proj_bias.shape[0]
    half = (d1 + LANES) // 2
    core = (lax.axis_index("seq") & 1).astype(jnp.int32).reshape(1)
    swap = [(i, i ^ 1) for i in range(members)]

    facing = [(i, i + 1 if i % 2 else i - 1) for i in range(1, members - 1)]

    hbm = pl.BlockSpec(memory_space=pltpu.HBM)
    gathered = (bases, embed_weight, embed_bias[None], norm_gain[None], proj_weight, proj_bias[None])
    piece, inner, outer = pl.pallas_call(
        pack_kernel,
        out_shape=(
            jax.ShapeDtypeStruct((shards, block, half), BF16),
            jax.ShapeDtypeStruct((1, LANES), jnp.int32),
            jax.ShapeDtypeStruct((1, LANES), jnp.int32),
        ),
        in_specs=[SMEM] + [hbm] * 6,
        out_specs=(VMEM,) * 3,
        scratch_shapes=[pltpu.VMEM(x.shape, x.dtype) for x in gathered] + [
            pltpu.VMEM((LANES, LANES), F32), pltpu.VMEM((block, LANES), F32), pltpu.SemaphoreType.DMA((6,))],
        compiler_params=pltpu.CompilerParams(vmem_limit_bytes=60 << 20),
        name="pack",
    )(core, *gathered)
    inner = lax.ppermute(inner, "seq", swap)
    outer = lax.ppermute(outer, "seq", facing)
    own = lax.all_to_all(piece, "dp", 0, 0, tiled=True).reshape(shards * block, half)
    feat, sums = make_features(core, inner, bases, outer, cotangent[0], kw, shards)
    own, feat, sums = lax.optimization_barrier((own, feat, sums))
    other = lax.ppermute(own, "seq", swap)

    cot = cotangent[0]
    theirs, s, wide, bias, w = backward(core, feat, sums, own, other, cot, kw, shards)
    came = lax.ppermute(theirs, "seq", swap)
    mine = keep_half(core, s, cot, wide, half)
    pooled = pool(s, w, bias)
    summed = (mine + came.astype(F32)).astype(BF16).reshape(shards, block, half)
    parts = lax.all_to_all(summed, "dp", 0, 0, tiled=True)

    def add_up(parts, scale, copies, kind):
        return pl.pallas_call(
            functools.partial(sum_kernel, scale),
            out_shape=jax.ShapeDtypeStruct((copies, block, half), kind),
            in_specs=[VMEM],
            out_specs=VMEM,
            compiler_params=pltpu.CompilerParams(vmem_limit_bytes=4 << 20),
            name="add_up",
        )(parts)

    groups = [[i + high for high in (0, 2) for i in range(c, members, 4)] for c in range(2)]
    spread = lax.all_to_all(add_up(parts, 1.0, members // 2, BF16), "seq", 0, 0, axis_index_groups=groups, tiled=True)
    total = add_up(spread, 0.125 / (cotangent.shape[1] * members * shards), 1, F32)[0]
    across = lax.ppermute(total, "seq", swap)
    grad_embed, grad_embed_bias, grad_gain, grad_proj, grad_proj_bias = pl.pallas_call(
        unpack_kernel,
        out_shape=(
            jax.ShapeDtypeStruct(embed_weight.shape, F32),
            jax.ShapeDtypeStruct((1, block), F32),
            jax.ShapeDtypeStruct((1, block), F32),
            jax.ShapeDtypeStruct((block, d1), F32),
            jax.ShapeDtypeStruct((1, per), F32),
        ),
        in_specs=[SMEM, VMEM, VMEM],
        out_specs=(VMEM,) * 5,
        scratch_shapes=[pltpu.VMEM((LANES, LANES), F32)],
        compiler_params=pltpu.CompilerParams(vmem_limit_bytes=4 << 20),
        name="unpack",
    )(core, total, across)
    return (pooled[None], grad_embed, grad_embed_bias[0], grad_gain[0], grad_proj, grad_proj_bias[0])


def solution(mesh):
    placed = (
        P("dp", "seq"),
        P(None, None, "dp"),
        P("dp"),
        P("dp"),
        P("dp", None),
        P("dp"),
        P("dp", "seq", None),
    )
    return jax.shard_map(
        local,
        mesh=mesh,
        in_specs=placed,
        out_specs=(
            P("dp", "seq", None),
            P(None, None, "dp"),
            P("dp"),
            P("dp"),
            P("dp", None),
            P("dp"),
        ),
        check_vma=False,
    )
```
